32 devices in a mesh: groups: 2 (over y), space: 4 (over x, core), tm: 4 (over z).
Axes of the slice: x: 2, y: 2, z: 4, core: 2. Of those that a mesh axis runs over, the one named last changes fastest.
Arguments:
- start_states: float32 [8, 64, 32, 128], P(('groups', 'tm'), None, 'space'), parts along dimension 0, may hold values from -6 to 6
- velocity: float32 [3, 64, 32, 128], P(None, None, 'space'), may hold values from -0.15 to 0.15
- diffusivity: float32 [64, 32, 128], P(None, 'space'), may hold values from 0.01 to 0.09
Outputs:
- corrected_ends: float32 [8, 64, 32, 128], P(('groups', 'tm'), None, 'space'), parts along dimension 0
- jumps: float32 [8, 64, 32, 128], P(('groups', 'tm'), None, 'space'), parts along dimension 0
The draws below stay inside these ranges and needn't reach their ends.
There are 2 independent parts, one for each index of `groups`. The reference program is written for one: setup_inputs(seed, part) draws one part's arguments, and reference() takes and returns one part's arrays. A program takes and returns all parts, laid end to end along the dimension named above; an argument that names none is the same for every part. Nothing has to cross between parts.
All inputs are finite; a program needn't handle non-finite values.
Results may differ from the reference program's by a relative error of at most 0.0001.
Values sent between devices are 32-bit elements; how exact they have to be, the bound alone decides.
No kernel may reach another device: no remote copies, remote signals or barrier semaphores. Data moves between devices by JAX's collectives and lax.ppermute only.
A program may use at most 128 MiB of HBM per device.

```python
import math
import jax
import jax.numpy as jnp

NZ = 64
NY = 128
FINE_STEPS = 2
SLICES = 4
NX = 32


def block_levels(rng, shape, cuts, smallest, high):
    def one(dim, parts):
        draws = jax.random.uniform(jax.random.fold_in(jax.random.fold_in(rng, 6), dim), (parts,), jnp.float32, smallest / len(cuts), high / len(cuts))
        return jnp.repeat(jnp.exp(draws), shape[dim] // parts).reshape((-1,) + (1,) * (len(shape) - dim - 1))

    gain = one(*cuts[0])
    for cut in cuts[1:]:
        gain = gain * one(*cut)
    return gain


def normal_values(rng, shape, scale, reach, pieces=(), dtype=jnp.bfloat16):
    values = scale * jax.random.normal(rng, shape, jnp.float32)
    if pieces:
        values = values * block_levels(rng, shape, pieces, -0.22, 0.18)
    return jnp.clip(values, -reach, reach).astype(dtype)


def setup_inputs(seed: int = 0, part: int = 0) -> dict:
    key_list = jax.random.split(jax.random.key(seed), 4)
    own_keys = jax.random.split(jax.random.fold_in(key_list[3], part), 4)
    return {
        "start_states": normal_values(own_keys[0], (SLICES, NZ, NX, NY), 1.0, 6.0, ((0, 4), (2, 4)), jnp.float32),
        "velocity": jnp.clip(jax.random.uniform(key_list[1], (3, NZ, NX, NY), jnp.float32, -0.15, 0.15) * block_levels(key_list[1], (3, NZ, NX, NY), ((2, 4),), -0.4, 0.0), -0.15, 0.15),
        "diffusivity": jnp.clip(jnp.exp(math.log(0.09) - 2.1972246 * jax.random.uniform(key_list[2], (NZ, NX, NY), jnp.float32) ** block_levels(key_list[2], (NZ, NX, NY), ((1, 4),), -0.2, 0.2)), 0.01, 0.09),
    }


def update(tracer, x_padded, coefficients):
    z_padded = jnp.pad(tracer, ((1, 1), (0, 0), (0, 0)))
    y_padded = jnp.pad(tracer, ((0, 0), (0, 0), (1, 1)))
    neighbours = ((z_padded[:-2], z_padded[2:]), (x_padded[:, :-2], x_padded[:, 2:]), (y_padded[:, :, :-2], y_padded[:, :, 2:]))
    diffusion = coefficients[3]
    updated = tracer
    for axis_number in range(3):
        lower_side, upper_side = neighbours[axis_number]
        speed_field = coefficients[axis_number]
        updated = updated - (jnp.maximum(speed_field, 0.0) * (tracer - lower_side) + jnp.minimum(speed_field, 0.0) * (upper_side - tracer)) + diffusion * (upper_side + lower_side - 2.0 * tracer)
    return updated


def pad_second(tracer):
    return jnp.pad(tracer, ((0, 0), (1, 1), (0, 0)))


def restrict(tracer):
    dims_now = tracer.shape
    reshaped = tracer.reshape(dims_now[:-3] + (dims_now[-3] // 4, 4, dims_now[-2] // 4, 4, dims_now[-1] // 4, 4))
    return jnp.mean(reshaped, axis=(-5, -3, -1))


def prolong(coarse):
    depth, rows, cols = coarse.shape
    spread = jnp.broadcast_to(coarse[:, None, :, None, :, None], (depth, 4, rows, 4, cols, 4))
    return spread.reshape(depth * 4, rows * 4, cols * 4)


def reference(start_states, velocity, diffusivity):
    coefficients = jnp.concatenate([velocity, diffusivity[None]], 0)
    coarse_scale = jnp.array([0.5, 0.5, 0.5, 0.125], jnp.float32)[:, None, None, None]
    coarse_coefficients = restrict(coefficients) * coarse_scale
    finished = []
    defects = []
    old_coarse = []
    for slice_index in range(SLICES):
        tracer = start_states[slice_index]
        for repeat in range(FINE_STEPS):
            tracer = update(tracer, pad_second(tracer), coefficients)
        coarse_start = restrict(start_states[slice_index])
        earlier = update(coarse_start, pad_second(coarse_start), coarse_coefficients)
        finished.append(tracer)
        old_coarse.append(earlier)
        defects.append(restrict(tracer) - earlier)
    current = restrict(start_states[0])
    corrected = []
    for slice_index in range(SLICES):
        imaged = update(current, pad_second(current), coarse_coefficients)
        corrected.append(finished[slice_index] + prolong(imaged - old_coarse[slice_index]))
        current = imaged + defects[slice_index]
    jump_list = [jnp.zeros_like(start_states[0])]
    for slice_index in range(1, SLICES):
        jump_list.append(start_states[slice_index] - finished[slice_index - 1])
    return jnp.stack(corrected), jnp.stack(jump_list)
```

```python
import jax
import jax.numpy as jnp
from jax import lax
from jax.experimental import pallas as pl
from jax.experimental.pallas import tpu as pltpu
from jax.sharding import PartitionSpec as P

NZ, ROWS, LANES = 64, 8, 128
FLAT = NZ * ROWS
CHUNK = 8
BITS = ((1, 1), (1, 2), (0, 1), (0, 2))

f32 = jnp.float32


def shifted(x, by, axis):
    return pltpu.roll(x, (-by) % x.shape[axis], axis)


def iotas(shape):
    n = len(shape)
    return (
        lax.broadcasted_iota(jnp.int32, shape, n - 2),
        lax.broadcasted_iota(jnp.int32, shape, n - 1),
    )


def restrict_tile(planes):
    sub, lane = iotas((ROWS, LANES))
    for axis, dist in BITS:
        low = ((lane if axis else sub) // dist) % 2 == 0
        planes = [
            jnp.where(low, a + shifted(a, dist, axis), b + shifted(b, -dist, axis))
            for a, b in zip(planes[0::2], planes[1::2])
        ]
    return planes[0]


def prolong_tile(tile):
    sub, lane = iotas((ROWS, LANES))
    planes = [tile]
    for axis, dist in reversed(BITS):
        low = ((lane if axis else sub) // dist) % 2 == 0
        grown = []
        for a in planes:
            grown.append(jnp.where(low, a, shifted(a, -dist, axis)))
            grown.append(jnp.where(low, shifted(a, dist, axis), a))
        planes = grown
    return planes


def plane_sums(ref):
    def one(c):
        at = c * 4 * ROWS
        return (ref[at : at + ROWS] + ref[at + ROWS : at + 2 * ROWS]) + (
            ref[at + 2 * ROWS : at + 3 * ROWS] + ref[at + 3 * ROWS : at + 4 * ROWS]
        )

    return [one(c) for c in range(NZ // 4)]


def weights(cz, cx, cy, diff):
    out = []
    for c in (cz, cx, cy):
        out.append(diff + jnp.maximum(c, 0.0))
        out.append(diff - jnp.minimum(c, 0.0))
    centre = 1.0 - ((out[0] + out[1]) + (out[2] + out[3]) + (out[4] + out[5]))
    return out + [centre]


def row(ref, at):
    return ref[pl.ds(at, NZ, stride=ROWS), :]


def local_kernel(v_ref, vel_ref, d_ref, q_ref, lo_ref, hi_ref, coarse_ref, keep_ref, rstart_ref, p_ref, pv_ref):
    zero = jnp.zeros((ROWS, LANES), f32)
    for ref in (p_ref, pv_ref):
        ref[0:ROWS] = zero
        ref[FLAT + ROWS : FLAT + 2 * ROWS] = zero
    pv_ref[ROWS : FLAT + ROWS] = v_ref[...]
    shape = (CHUNK, ROWS, LANES)
    sub, lane = iotas(shape)
    size = CHUNK * ROWS

    def step(src, dst, dst_off):
        def body(c, carry):
            at = pl.multiple_of(c * size, size)
            load = lambda ref, off: ref[pl.ds(at + off, size), :].reshape(shape)
            w = weights(
                load(vel_ref, 0), load(vel_ref, FLAT), load(vel_ref, 2 * FLAT), load(d_ref, 0)
            )
            v = load(src, ROWS)
            total = w[6] * v + w[0] * load(src, 0) + w[1] * load(src, 2 * ROWS)
            total += jnp.where(sub == 0, 0.0, w[2]) * shifted(v, -1, 1)
            total += jnp.where(sub == ROWS - 1, 0.0, w[3]) * shifted(v, 1, 1)
            total += jnp.where(lane == 0, 0.0, w[4]) * shifted(v, -1, 2)
            total += jnp.where(lane == LANES - 1, 0.0, w[5]) * shifted(v, 1, 2)
            dst[pl.ds(at + dst_off, size), :] = total.reshape(size, LANES)
            return carry

        lax.fori_loop(0, NZ // CHUNK, body, 0)

    step(pv_ref, p_ref, ROWS)
    diff0, diff7 = row(d_ref, 0), row(d_ref, ROWS - 1)
    cx0, cx7 = row(vel_ref, FLAT), row(vel_ref, FLAT + ROWS - 1)
    k0 = diff0 + jnp.maximum(cx0, 0.0)
    k7 = diff7 - jnp.minimum(cx7, 0.0)
    lo_ref[0:NZ] = row(v_ref, 0)
    lo_ref[NZ : 2 * NZ] = row(p_ref, ROWS)
    lo_ref[2 * NZ : 3 * NZ] = k0
    hi_ref[0:NZ] = row(v_ref, ROWS - 1)
    hi_ref[NZ : 2 * NZ] = row(p_ref, 2 * ROWS - 1)
    hi_ref[2 * NZ : 3 * NZ] = k7
    for side, at in enumerate((0, ROWS - 1)):
        w = weights(*(row(vel_ref, d * FLAT + at) for d in range(3)), row(d_ref, at))
        for j, value in enumerate((w[0], w[1], w[4], w[5], w[6])):
            keep_ref[(side * 6 + j) * NZ : (side * 6 + j + 1) * NZ] = value
    keep_ref[5 * NZ : 6 * NZ] = row(d_ref, 1) + jnp.maximum(row(vel_ref, FLAT + 1), 0.0)
    keep_ref[11 * NZ : 12 * NZ] = row(d_ref, ROWS - 2) - jnp.minimum(row(vel_ref, FLAT + ROWS - 2), 0.0)
    step(p_ref, q_ref, 0)
    for d in range(3):
        sums = restrict_tile(plane_sums(vel_ref.at[d * FLAT : (d + 1) * FLAT]))
        coarse_ref[d] = sums * (0.5 / 64)
    coarse_ref[3] = restrict_tile(plane_sums(d_ref)) * (0.125 / 64)
    rstart_ref[...] = restrict_tile(plane_sums(v_ref)) * (1.0 / 64)


def finish_kernel(parts, place_ref, q_ref, lo_ref, hi_ref, fromlow_ref, fromhigh_ref, keep_ref, nextstart_ref, fine_ref, tiles_ref):
    has_low = place_ref[0] > 0
    has_high = place_ref[1] > 0
    part = lambda ref, j: ref[j * NZ : (j + 1) * NZ]
    sub, lane = iotas((NZ, LANES))
    fine_ref[...] = q_ref[...]
    for side in range(2):
        far, own, there = (
            (fromlow_ref, lo_ref, has_low) if side == 0 else (fromhigh_ref, hi_ref, has_high)
        )
        wbz, waz, wby, way, centre, inner = (part(keep_ref, side * 6 + j) for j in range(6))
        k = jnp.where(there, part(own, 2), 0.0)
        delta = k * part(far, 0)
        beyond = part(far, 1) + part(far, 2) * part(own, 0)
        edge = centre * delta + k * beyond
        edge += jnp.where(sub == 0, 0.0, wbz) * shifted(delta, -1, 0)
        edge += jnp.where(sub == NZ - 1, 0.0, waz) * shifted(delta, 1, 0)
        edge += jnp.where(lane == 0, 0.0, wby) * shifted(delta, -1, 1)
        edge += jnp.where(lane == LANES - 1, 0.0, way) * shifted(delta, 1, 1)
        e_at, i_at = (0, 1) if side == 0 else (ROWS - 1, ROWS - 2)
        fine_ref[pl.ds(e_at, NZ, stride=ROWS), :] = row(q_ref, e_at) + edge
        fine_ref[pl.ds(i_at, NZ, stride=ROWS), :] = row(q_ref, i_at) + inner * delta
    tile = restrict_tile(plane_sums(fine_ref)) * (1.0 / 64) - nextstart_ref[...]
    for j in range(parts):
        tiles_ref[j] = tile


def sweep_kernel(bricks, slices, place_ref, jumps_ref, *refs):
    coarse_refs = refs[:bricks]
    fine_ref, earlier_ref, start_ref, corrected_ref, jump_ref, change_ref = refs[bricks:]
    own, n = place_ref[0], place_ref[1]
    sub, lane = iotas((ROWS, LANES))
    zl, zh, y = lane % 4, sub % 4, lane // 4
    w = []
    for b in range(bricks):
        c = coarse_refs[b]
        wb = weights(c[0], c[1], c[2], c[3])
        wb[0] = jnp.where((zl == 0) & (zh == 0), 0.0, wb[0])
        wb[1] = jnp.where((zl == 3) & (zh == 3), 0.0, wb[1])
        wb[4] = jnp.where(y == 0, 0.0, wb[4])
        wb[5] = jnp.where(y == LANES // 4 - 1, 0.0, wb[5])
        if b == 0:
            wb[2] = jnp.where(sub < 4, 0.0, wb[2])
        if b == bricks - 1:
            wb[3] = jnp.where(sub < 4, wb[3], 0.0)
        w.append(wb)

    def coarse_step(m, change):
        e = [change[b] + jumps_ref[b * slices + m] for b in range(bricks)]
        half = [shifted(v, 4, 0) for v in e]
        out = []
        for b in range(bricks):
            v = e[b]
            lower = half[max(b - 1, 0)]
            upper = half[min(b + 1, bricks - 1)]
            zb = jnp.where(zl == 0, shifted(shifted(v, 3, 1), -1, 0), shifted(v, -1, 1))
            za = jnp.where(zl == 3, shifted(shifted(v, -3, 1), 1, 0), shifted(v, 1, 1))
            xb = jnp.where(sub < 4, lower, half[b])
            xa = jnp.where(sub < 4, half[b], upper)
            out.append(
                (w[b][6] * v + w[b][0] * zb + w[b][1] * za)
                + (w[b][2] * xb + w[b][3] * xa)
                + (w[b][4] * shifted(v, -4, 1) + w[b][5] * shifted(v, 4, 1))
            )
        return tuple(out)

    zero = tuple(jnp.zeros((ROWS, LANES), f32) for _ in range(bricks))
    change = lax.fori_loop(0, n, coarse_step, zero)
    for b in range(bricks):
        change_ref[b] = change[b]
    planes = prolong_tile(change_ref[own])
    for z in range(NZ):
        at = slice(z * ROWS, (z + 1) * ROWS)
        corrected_ref[at] = fine_ref[at] + planes[z // 4]
    first = n == 0
    jump_ref[...] = jnp.where(first, 0.0, start_ref[...] - earlier_ref[...])


def local(start_states, velocity, diffusivity):
    bricks, slices = lax.axis_size("space"), lax.axis_size("tm")
    own, n = lax.axis_index("space"), lax.axis_index("tm")
    start = start_states.reshape(FLAT, LANES)
    sds = lambda *shape: jax.ShapeDtypeStruct(shape, f32)
    ring = lambda count, by: [(i, (i + by) % count) for i in range(count)]
    vmem = pl.BlockSpec(memory_space=pltpu.VMEM)
    smem = pl.BlockSpec(memory_space=pltpu.SMEM)

    q, lo, hi, coarse, keep, rstart = pl.pallas_call(
        local_kernel,
        in_specs=[vmem] * 3,
        out_specs=[vmem] * 6,
        out_shape=[
            sds(FLAT, LANES),
            sds(3 * NZ, LANES),
            sds(3 * NZ, LANES),
            sds(4, ROWS, LANES),
            sds(12 * NZ, LANES),
            sds(ROWS, LANES),
        ],
        scratch_shapes=[pltpu.VMEM((FLAT + 2 * ROWS, LANES), f32)] * 2,
        name="local_steps",
    )(start, velocity.reshape(3 * FLAT, LANES), diffusivity.reshape(FLAT, LANES))

    fromlow = lax.ppermute(hi, "space", ring(bricks, 1))
    fromhigh = lax.ppermute(lo, "space", ring(bricks, bricks - 1))
    nextstart = lax.ppermute(rstart, "tm", ring(slices, slices - 1))
    coarse_all = lax.all_gather(coarse, "space")

    edges = jnp.stack([own, bricks - 1 - own]).astype(jnp.int32)
    fine, tiles = pl.pallas_call(
        lambda *refs: finish_kernel(bricks * slices, *refs),
        in_specs=[smem] + [vmem] * 7,
        out_specs=[vmem] * 2,
        out_shape=[sds(FLAT, LANES), sds(bricks * slices, ROWS, LANES)],
        name="finish_steps",
    )(edges, q, lo, hi, fromlow, fromhigh, keep, nextstart)

    earlier = lax.ppermute(fine, "tm", ring(slices, 1))
    jumps = lax.all_to_all(tiles, ("space", "tm"), 0, 0)

    place = jnp.stack([own, n]).astype(jnp.int32)
    corrected, jump = pl.pallas_call(
        lambda *refs: sweep_kernel(bricks, slices, *refs),
        in_specs=[smem] + [vmem] * (bricks + 4),
        out_specs=[vmem] * 2,
        out_shape=[sds(FLAT, LANES)] * 2,
        scratch_shapes=[pltpu.VMEM((bricks, ROWS, LANES), f32)],
        name="sweep",
    )(place, jumps, *[coarse_all[b] for b in range(bricks)], fine, earlier, start)
    shape = (1, NZ, ROWS, LANES)
    return corrected.reshape(shape), jump.reshape(shape)


def solution(mesh):
    in_specs = (
        P(("groups", "tm"), None, "space", None),
        P(None, None, "space", None),
        P(None, "space", None),
    )
    out_specs = (P(("groups", "tm"), None, "space", None), P(("groups", "tm"), None, "space", None))
    return jax.shard_map(local, mesh=mesh, in_specs=in_specs, out_specs=out_specs, check_vma=False)
```

```python
import jax
import jax.numpy as jnp
from jax import lax
from jax.experimental import pallas as pl
from jax.experimental.pallas import tpu as pltpu
from jax.sharding import PartitionSpec as P

NZ, ROWS, LANES = 64, 8, 128
FLAT = NZ * ROWS
CHUNK = 8
BITS = ((1, 1), (1, 2), (0, 1), (0, 2))

f32 = jnp.float32


def shifted(x, by, axis):
    return pltpu.roll(x, (-by) % x.shape[axis], axis)


def iotas(shape):
    n = len(shape)
    return (
        lax.broadcasted_iota(jnp.int32, shape, n - 2),
        lax.broadcasted_iota(jnp.int32, shape, n - 1),
    )


def restrict_tile(planes):
    sub, lane = iotas((ROWS, LANES))
    for axis, dist in BITS:
        low = ((lane if axis else sub) // dist) % 2 == 0
        planes = [
            jnp.where(low, a + shifted(a, dist, axis), b + shifted(b, -dist, axis))
            for a, b in zip(planes[0::2], planes[1::2])
        ]
    return planes[0]


def prolong_tile(tile):
    sub, lane = iotas((ROWS, LANES))
    planes = [tile]
    for axis, dist in reversed(BITS):
        low = ((lane if axis else sub) // dist) % 2 == 0
        grown = []
        for a in planes:
            grown.append(jnp.where(low, a, shifted(a, -dist, axis)))
            grown.append(jnp.where(low, shifted(a, dist, axis), a))
        planes = grown
    return planes


def plane_sums(ref):
    def one(c):
        at = c * 4 * ROWS
        return (ref[at : at + ROWS] + ref[at + ROWS : at + 2 * ROWS]) + (
            ref[at + 2 * ROWS : at + 3 * ROWS] + ref[at + 3 * ROWS : at + 4 * ROWS]
        )

    return [one(c) for c in range(NZ // 4)]


def weights(cz, cx, cy, diff):
    out = []
    for c in (cz, cx, cy):
        out.append(diff + jnp.maximum(c, 0.0))
        out.append(diff - jnp.minimum(c, 0.0))
    centre = 1.0 - ((out[0] + out[1]) + (out[2] + out[3]) + (out[4] + out[5]))
    return out + [centre]


def row(ref, at):
    return ref[pl.ds(at, NZ, stride=ROWS), :]


def edges_kernel(v_hbm, vel_hbm, d_hbm, v_ref, vel_ref, d_ref, lo_ref, hi_ref, sems):
    copies = [
        pltpu.make_async_copy(src, dst, sems.at[i])
        for i, (src, dst) in enumerate(((v_hbm, v_ref), (d_hbm, d_ref), (vel_hbm, vel_ref)))
    ]
    for copy in copies:
        copy.start()
    for copy in copies:
        copy.wait()
    sub, lane = iotas((NZ, LANES))
    for out, face, inner, side in ((lo_ref, 0, 1, 0), (hi_ref, ROWS - 1, ROWS - 2, 1)):
        w = weights(*(row(vel_ref, d * FLAT + face) for d in range(3)), row(d_ref, face))
        v = row(v_ref, face)
        total = w[6] * v + w[3 - side] * row(v_ref, inner)
        total += jnp.where(sub == 0, 0.0, w[0]) * shifted(v, -1, 0)
        total += jnp.where(sub == NZ - 1, 0.0, w[1]) * shifted(v, 1, 0)
        total += jnp.where(lane == 0, 0.0, w[4]) * shifted(v, -1, 1)
        total += jnp.where(lane == LANES - 1, 0.0, w[5]) * shifted(v, 1, 1)
        out[0:NZ] = v
        out[NZ : 2 * NZ] = total
        out[2 * NZ : 3 * NZ] = w[2 + side]


def steps_kernel(v_ref, vel_ref, d_ref, q_ref, coarse_ref, keep_ref, rstart_ref, p_ref, pv_ref):
    zero = jnp.zeros((ROWS, LANES), f32)
    for ref in (p_ref, pv_ref):
        ref[0:ROWS] = zero
        ref[FLAT + ROWS : FLAT + 2 * ROWS] = zero
    pv_ref[ROWS : FLAT + ROWS] = v_ref[...]
    shape = (CHUNK, ROWS, LANES)
    sub, lane = iotas(shape)
    size = CHUNK * ROWS

    def step(src, dst, dst_off):
        def body(c, carry):
            at = pl.multiple_of(c * size, size)
            load = lambda ref, off: ref[pl.ds(at + off, size), :].reshape(shape)
            w = weights(
                load(vel_ref, 0), load(vel_ref, FLAT), load(vel_ref, 2 * FLAT), load(d_ref, 0)
            )
            v = load(src, ROWS)
            total = w[6] * v + w[0] * load(src, 0) + w[1] * load(src, 2 * ROWS)
            total += jnp.where(sub == 0, 0.0, w[2]) * shifted(v, -1, 1)
            total += jnp.where(sub == ROWS - 1, 0.0, w[3]) * shifted(v, 1, 1)
            total += jnp.where(lane == 0, 0.0, w[4]) * shifted(v, -1, 2)
            total += jnp.where(lane == LANES - 1, 0.0, w[5]) * shifted(v, 1, 2)
            dst[pl.ds(at + dst_off, size), :] = total.reshape(size, LANES)
            return carry

        lax.fori_loop(0, NZ // CHUNK, body, 0)

    step(pv_ref, p_ref, ROWS)
    step(p_ref, q_ref, 0)
    for side, at in enumerate((0, ROWS - 1)):
        w = weights(*(row(vel_ref, d * FLAT + at) for d in range(3)), row(d_ref, at))
        for j, value in enumerate((w[0], w[1], w[4], w[5], w[6])):
            keep_ref[(side * 6 + j) * NZ : (side * 6 + j + 1) * NZ] = value
    keep_ref[5 * NZ : 6 * NZ] = row(d_ref, 1) + jnp.maximum(row(vel_ref, FLAT + 1), 0.0)
    keep_ref[11 * NZ : 12 * NZ] = row(d_ref, ROWS - 2) - jnp.minimum(row(vel_ref, FLAT + ROWS - 2), 0.0)
    for d in range(3):
        sums = restrict_tile(plane_sums(vel_ref.at[d * FLAT : (d + 1) * FLAT]))
        coarse_ref[d] = sums * (0.5 / 64)
    coarse_ref[3] = restrict_tile(plane_sums(d_ref)) * (0.125 / 64)
    rstart_ref[...] = restrict_tile(plane_sums(v_ref)) * (1.0 / 64)


def finish_kernel(parts, bricks, q_ref, lo_ref, hi_ref, fromlow_ref, fromhigh_ref, keep_ref, rstart_ref, fine_ref, tiles_ref):
    own_brick = lax.axis_index("space")
    has_low = own_brick > 0
    has_high = own_brick < bricks - 1
    part = lambda ref, j: ref[j * NZ : (j + 1) * NZ]
    sub, lane = iotas((NZ, LANES))
    fine_ref[...] = q_ref[...]
    for side in range(2):
        far, own, there = (
            (fromlow_ref, lo_ref, has_low) if side == 0 else (fromhigh_ref, hi_ref, has_high)
        )
        wbz, waz, wby, way, centre, inner = (part(keep_ref, side * 6 + j) for j in range(6))
        k = jnp.where(there, part(own, 2), 0.0)
        delta = k * part(far, 0)
        beyond = part(far, 1) + part(far, 2) * part(own, 0)
        edge = centre * delta + k * beyond
        edge += jnp.where(sub == 0, 0.0, wbz) * shifted(delta, -1, 0)
        edge += jnp.where(sub == NZ - 1, 0.0, waz) * shifted(delta, 1, 0)
        edge += jnp.where(lane == 0, 0.0, wby) * shifted(delta, -1, 1)
        edge += jnp.where(lane == LANES - 1, 0.0, way) * shifted(delta, 1, 1)
        e_at, i_at = (0, 1) if side == 0 else (ROWS - 1, ROWS - 2)
        fine_ref[pl.ds(e_at, NZ, stride=ROWS), :] = row(q_ref, e_at) + edge
        fine_ref[pl.ds(i_at, NZ, stride=ROWS), :] = row(q_ref, i_at) + inner * delta
    tile = restrict_tile(plane_sums(fine_ref)) * (1.0 / 64)
    rstart = rstart_ref[...]
    for j in range(parts):
        tiles_ref[j, 0:ROWS] = tile
        tiles_ref[j, ROWS : 2 * ROWS] = rstart


def jump_kernel(earlier_ref, start_ref, jump_ref):
    first = lax.axis_index("tm") == 0
    jump_ref[...] = jnp.where(first, 0.0, start_ref[...] - earlier_ref[...])


def sweep_kernel(bricks, slices, images_ref, fine_ref, *refs):
    coarse_refs = refs[:bricks]
    corrected_ref, change_ref, coef_ref = refs[bricks:]
    own, n = lax.axis_index("space"), lax.axis_index("tm")
    for k in range(bricks):
        coef_ref[(own + bricks - k) % bricks] = coarse_refs[k][...]
    sub, lane = iotas((ROWS, LANES))
    zl, zh, y = lane % 4, sub % 4, lane // 4
    w = []
    for b in range(bricks):
        c = coef_ref.at[b]
        wb = weights(c[0], c[1], c[2], c[3])
        wb[0] = jnp.where((zl == 0) & (zh == 0), 0.0, wb[0])
        wb[1] = jnp.where((zl == 3) & (zh == 3), 0.0, wb[1])
        wb[4] = jnp.where(y == 0, 0.0, wb[4])
        wb[5] = jnp.where(y == LANES // 4 - 1, 0.0, wb[5])
        if b == 0:
            wb[2] = jnp.where(sub < 4, 0.0, wb[2])
        if b == bricks - 1:
            wb[3] = jnp.where(sub < 4, wb[3], 0.0)
        w.append(wb)

    def coarse_step(m, change):
        e = [
            change[b] + (images_ref[b * slices + m, 0:ROWS] - images_ref[b * slices + m + 1, ROWS : 2 * ROWS])
            for b in range(bricks)
        ]
        half = [shifted(v, 4, 0) for v in e]
        out = []
        for b in range(bricks):
            v = e[b]
            lower = half[max(b - 1, 0)]
            upper = half[min(b + 1, bricks - 1)]
            zb = jnp.where(zl == 0, shifted(shifted(v, 3, 1), -1, 0), shifted(v, -1, 1))
            za = jnp.where(zl == 3, shifted(shifted(v, -3, 1), 1, 0), shifted(v, 1, 1))
            xb = jnp.where(sub < 4, lower, half[b])
            xa = jnp.where(sub < 4, half[b], upper)
            out.append(
                (w[b][6] * v + w[b][0] * zb + w[b][1] * za)
                + (w[b][2] * xb + w[b][3] * xa)
                + (w[b][4] * shifted(v, -4, 1) + w[b][5] * shifted(v, 4, 1))
            )
        return tuple(out)

    zero = tuple(jnp.zeros((ROWS, LANES), f32) for _ in range(bricks))
    change = lax.fori_loop(0, n, coarse_step, zero)
    for b in range(bricks):
        change_ref[b] = change[b]
    planes = prolong_tile(change_ref[own])
    for z in range(NZ):
        at = slice(z * ROWS, (z + 1) * ROWS)
        corrected_ref[at] = fine_ref[at] + planes[z // 4]


def local(start_states, velocity, diffusivity):
    bricks, slices = lax.axis_size("space"), lax.axis_size("tm")
    parts = bricks * slices
    ring = lambda count, by: [(i, (i + by) % count) for i in range(count)]
    out = lambda *shape: pltpu.VMEM(shape, f32)
    vmem, anyspace = pl.BlockSpec(memory_space=pltpu.VMEM), pl.BlockSpec(memory_space=pl.ANY)
    inside = lambda *xs: [pltpu.with_memory_space_constraint(x, pltpu.VMEM) for x in xs]

    v, vel, diff, lo, hi = pl.pallas_call(
        edges_kernel,
        in_specs=[anyspace] * 3,
        out_specs=[vmem] * 5,
        out_shape=[
            out(FLAT, LANES),
            out(3 * FLAT, LANES),
            out(FLAT, LANES),
            out(3 * NZ, LANES),
            out(3 * NZ, LANES),
        ],
        scratch_shapes=[pltpu.SemaphoreType.DMA((3,))],
        name="edges",
    )(
        start_states.reshape(FLAT, LANES),
        velocity.reshape(3 * FLAT, LANES),
        diffusivity.reshape(FLAT, LANES),
    )
    fromlow = lax.ppermute(hi, "space", ring(bricks, 1))
    fromhigh = lax.ppermute(lo, "space", ring(bricks, bricks - 1))

    q, coarse, keep, rstart = pl.pallas_call(
        steps_kernel,
        in_specs=[vmem] * 3,
        out_specs=[vmem] * 4,
        out_shape=[
            out(FLAT, LANES),
            out(4, ROWS, LANES),
            out(12 * NZ, LANES),
            out(ROWS, LANES),
        ],
        scratch_shapes=[pltpu.VMEM((FLAT + 2 * ROWS, LANES), f32)] * 2,
        name="steps",
    )(*inside(v, vel, diff))

    fine, tiles = pl.pallas_call(
        lambda *refs: finish_kernel(parts, bricks, *refs),
        in_specs=[vmem] * 7,
        out_specs=[vmem] * 2,
        out_shape=[out(FLAT, LANES), out(parts, 2 * ROWS, LANES)],
        name="finish",
    )(*inside(q, lo, hi, fromlow, fromhigh, keep, rstart))

    earlier = lax.ppermute(fine, "tm", ring(slices, 1))
    images = lax.all_to_all(tiles, ("space", "tm"), 0, 0)
    coarse_all = [coarse] + [lax.ppermute(coarse, "space", ring(bricks, k)) for k in range(1, bricks)]

    jump = pl.pallas_call(
        jump_kernel,
        in_specs=[vmem] * 2,
        out_specs=vmem,
        out_shape=jax.ShapeDtypeStruct((FLAT, LANES), f32),
        name="jump",
    )(*inside(earlier, v))

    corrected = pl.pallas_call(
        lambda *refs: sweep_kernel(bricks, slices, *refs),
        in_specs=[vmem] * (bricks + 2),
        out_specs=vmem,
        out_shape=jax.ShapeDtypeStruct((FLAT, LANES), f32),
        scratch_shapes=[
            pltpu.VMEM((bricks, ROWS, LANES), f32),
            pltpu.VMEM((bricks, 4, ROWS, LANES), f32),
        ],
        name="sweep",
    )(*inside(images, fine, *coarse_all))
    shape = (1, NZ, ROWS, LANES)
    return corrected.reshape(shape), jump.reshape(shape)


def solution(mesh):
    in_specs = (
        P(("groups", "tm"), None, "space", None),
        P(None, None, "space", None),
        P(None, "space", None),
    )
    out_specs = (P(("groups", "tm"), None, "space", None), P(("groups", "tm"), None, "space", None))
    return jax.shard_map(local, mesh=mesh, in_specs=in_specs, out_specs=out_specs, check_vma=False)
```

```python
import jax
import jax.numpy as jnp
from jax import lax
from jax.experimental import pallas as pl
from jax.experimental.pallas import tpu as pltpu
from jax.sharding import PartitionSpec as P

NZ, ROWS, LANES = 64, 8, 128
FLAT = NZ * ROWS
CHUNK = 8
BITS = ((1, 1), (1, 2), (0, 1), (0, 2))

f32 = jnp.float32


def shifted(x, by, axis):
    return pltpu.roll(x, (-by) % x.shape[axis], axis)


def iotas(shape):
    n = len(shape)
    return (
        lax.broadcasted_iota(jnp.int32, shape, n - 2),
        lax.broadcasted_iota(jnp.int32, shape, n - 1),
    )


def restrict_tile(planes):
    sub, lane = iotas((ROWS, LANES))
    for axis, dist in BITS:
        low = ((lane if axis else sub) // dist) % 2 == 0
        planes = [
            jnp.where(low, a + shifted(a, dist, axis), b + shifted(b, -dist, axis))
            for a, b in zip(planes[0::2], planes[1::2])
        ]
    return planes[0]


def prolong_tile(tile):
    sub, lane = iotas((ROWS, LANES))
    planes = [tile]
    for axis, dist in reversed(BITS):
        low = ((lane if axis else sub) // dist) % 2 == 0
        grown = []
        for a in planes:
            grown.append(jnp.where(low, a, shifted(a, -dist, axis)))
            grown.append(jnp.where(low, shifted(a, dist, axis), a))
        planes = grown
    return planes


def plane_sums(ref):
    def one(c):
        at = c * 4 * ROWS
        return (ref[at : at + ROWS] + ref[at + ROWS : at + 2 * ROWS]) + (
            ref[at + 2 * ROWS : at + 3 * ROWS] + ref[at + 3 * ROWS : at + 4 * ROWS]
        )

    return [one(c) for c in range(NZ // 4)]


def weights(cz, cx, cy, diff):
    out = []
    for c in (cz, cx, cy):
        out.append(diff + jnp.maximum(c, 0.0))
        out.append(diff - jnp.minimum(c, 0.0))
    centre = 1.0 - ((out[0] + out[1]) + (out[2] + out[3]) + (out[4] + out[5]))
    return out + [centre]


def row(ref, at):
    return ref[pl.ds(at, NZ, stride=ROWS), :]


def edges_kernel(v_hbm, vel_hbm, d_hbm, v_ref, vel_ref, d_ref, pair_ref, cross_ref, sems):
    copies = [
        pltpu.make_async_copy(src, dst, sems.at[i])
        for i, (src, dst) in enumerate(((v_hbm, v_ref), (d_hbm, d_ref), (vel_hbm, vel_ref)))
    ]
    for copy in copies:
        copy.start()
    copies[0].wait()
    odd = lax.axis_index("space") % 2 == 1
    image = restrict_tile(plane_sums(v_ref)) * (1.0 / 64)
    for copy in copies[1:]:
        copy.wait()
    sub, lane = iotas((NZ, LANES))
    rows = []
    for face, inner, side in ((0, 1, 0), (ROWS - 1, ROWS - 2, 1)):
        w = weights(*(row(vel_ref, d * FLAT + face) for d in range(3)), row(d_ref, face))
        v = row(v_ref, face)
        total = w[6] * v + w[3 - side] * row(v_ref, inner)
        total += jnp.where(sub == 0, 0.0, w[0]) * shifted(v, -1, 0)
        total += jnp.where(sub == NZ - 1, 0.0, w[1]) * shifted(v, 1, 0)
        total += jnp.where(lane == 0, 0.0, w[4]) * shifted(v, -1, 1)
        total += jnp.where(lane == LANES - 1, 0.0, w[5]) * shifted(v, 1, 1)
        rows.append((v, total, w[2 + side]))
    for j, (low, high) in enumerate(zip(*rows)):
        pair_ref[j * NZ : (j + 1) * NZ] = jnp.where(odd, low, high)
        cross_ref[j * NZ : (j + 1) * NZ] = jnp.where(odd, high, low)
    for ref in (pair_ref, cross_ref):
        ref[3 * NZ : 3 * NZ + ROWS] = image


def steps_kernel(v_ref, vel_ref, d_ref, q_ref, coarse_ref, keep_ref, p_ref, pv_ref):
    zero = jnp.zeros((ROWS, LANES), f32)
    for ref in (p_ref, pv_ref):
        ref[0:ROWS] = zero
        ref[FLAT + ROWS : FLAT + 2 * ROWS] = zero
    pv_ref[ROWS : FLAT + ROWS] = v_ref[...]
    shape = (CHUNK, ROWS, LANES)
    sub, lane = iotas(shape)
    size = CHUNK * ROWS

    def step(src, dst, dst_off):
        def body(c, carry):
            at = pl.multiple_of(c * size, size)
            load = lambda ref, off: ref[pl.ds(at + off, size), :].reshape(shape)
            w = weights(
                load(vel_ref, 0), load(vel_ref, FLAT), load(vel_ref, 2 * FLAT), load(d_ref, 0)
            )
            v = load(src, ROWS)
            total = w[6] * v + w[0] * load(src, 0) + w[1] * load(src, 2 * ROWS)
            total += jnp.where(sub == 0, 0.0, w[2]) * shifted(v, -1, 1)
            total += jnp.where(sub == ROWS - 1, 0.0, w[3]) * shifted(v, 1, 1)
            total += jnp.where(lane == 0, 0.0, w[4]) * shifted(v, -1, 2)
            total += jnp.where(lane == LANES - 1, 0.0, w[5]) * shifted(v, 1, 2)
            dst[pl.ds(at + dst_off, size), :] = total.reshape(size, LANES)
            return carry

        lax.fori_loop(0, NZ // CHUNK, body, 0)

    step(pv_ref, p_ref, ROWS)
    step(p_ref, q_ref, 0)
    for side, at in enumerate((0, ROWS - 1)):
        w = weights(*(row(vel_ref, d * FLAT + at) for d in range(3)), row(d_ref, at))
        for j, value in enumerate((w[0], w[1], w[4], w[5], w[6])):
            keep_ref[(side * 6 + j) * NZ : (side * 6 + j + 1) * NZ] = value
    keep_ref[5 * NZ : 6 * NZ] = row(d_ref, 1) + jnp.maximum(row(vel_ref, FLAT + 1), 0.0)
    keep_ref[11 * NZ : 12 * NZ] = row(d_ref, ROWS - 2) - jnp.minimum(row(vel_ref, FLAT + ROWS - 2), 0.0)
    for d in range(3):
        sums = restrict_tile(plane_sums(vel_ref.at[d * FLAT : (d + 1) * FLAT]))
        coarse_ref[d] = sums * (0.5 / 64)
    coarse_ref[3] = restrict_tile(plane_sums(d_ref)) * (0.125 / 64)


def coarse_weights(c, first, last):
    sub, lane = iotas((ROWS, LANES))
    zl, zh, y = lane % 4, sub % 4, lane // 4
    w = weights(c[0], c[1], c[2], c[3])
    w[0] = jnp.where((zl == 0) & (zh == 0), 0.0, w[0])
    w[1] = jnp.where((zl == 3) & (zh == 3), 0.0, w[1])
    w[4] = jnp.where(y == 0, 0.0, w[4])
    w[5] = jnp.where(y == LANES // 4 - 1, 0.0, w[5])
    w[2] = jnp.where((sub < 4) & first, 0.0, w[2])
    w[3] = jnp.where((sub >= 4) & last, 0.0, w[3])
    return w


def coarse_apply(w, v, own, lower, upper):
    sub, lane = iotas((ROWS, LANES))
    zl = lane % 4
    zb = jnp.where(zl == 0, shifted(shifted(v, 3, 1), -1, 0), shifted(v, -1, 1))
    za = jnp.where(zl == 3, shifted(shifted(v, -3, 1), 1, 0), shifted(v, 1, 1))
    xb = jnp.where(sub < 4, lower, own)
    xa = jnp.where(sub < 4, own, upper)
    return (
        (w[6] * v + w[0] * zb + w[1] * za)
        + (w[2] * xb + w[3] * xa)
        + (w[4] * shifted(v, -4, 1) + w[5] * shifted(v, 4, 1))
    )


def finish_kernel(parts, bricks, q_ref, mine_pair_ref, mine_cross_ref, pair_ref, cross_ref, keep_ref, coarse_ref, fine_ref, tiles_ref, old_ref):
    brick = lax.axis_index("space")
    odd = brick % 2 == 1
    has_low = brick > 0
    has_high = brick < bricks - 1
    part = lambda ref, j: ref[j * NZ : (j + 1) * NZ]

    def sides(pair, cross, j):
        a, b = part(pair, j), part(cross, j)
        return jnp.where(odd, a, b), jnp.where(odd, b, a)

    own = [sides(mine_pair_ref, mine_cross_ref, j) for j in (0, 2)]
    far = [sides(pair_ref, cross_ref, j) for j in range(3)]
    sub, lane = iotas((NZ, LANES))
    fine_ref[...] = q_ref[...]
    for side in range(2):
        wbz, waz, wby, way, centre, inner = (part(keep_ref, side * 6 + j) for j in range(6))
        k = jnp.where(has_high if side else has_low, own[1][side], 0.0)
        delta = k * far[0][side]
        beyond = far[1][side] + far[2][side] * own[0][side]
        edge = centre * delta + k * beyond
        edge += jnp.where(sub == 0, 0.0, wbz) * shifted(delta, -1, 0)
        edge += jnp.where(sub == NZ - 1, 0.0, waz) * shifted(delta, 1, 0)
        edge += jnp.where(lane == 0, 0.0, wby) * shifted(delta, -1, 1)
        edge += jnp.where(lane == LANES - 1, 0.0, way) * shifted(delta, 1, 1)
        e_at, i_at = (0, 1) if side == 0 else (ROWS - 1, ROWS - 2)
        fine_ref[pl.ds(e_at, NZ, stride=ROWS), :] = row(q_ref, e_at) + edge
        fine_ref[pl.ds(i_at, NZ, stride=ROWS), :] = row(q_ref, i_at) + inner * delta
    at = slice(3 * NZ, 3 * NZ + ROWS)
    v = mine_pair_ref[at]
    lower = jnp.where(odd, pair_ref[at], cross_ref[at])
    upper = jnp.where(odd, cross_ref[at], pair_ref[at])
    w = coarse_weights(coarse_ref, jnp.logical_not(has_low), jnp.logical_not(has_high))
    old = coarse_apply(w, v, *(shifted(x, 4, 0) for x in (v, lower, upper)))
    old_ref[...] = old
    image = restrict_tile(plane_sums(fine_ref)) * (1.0 / 64)
    tile = jnp.where(lax.axis_index("tm") == 0, image, image - old)
    for j in range(parts):
        tiles_ref[j] = tile


def jump_kernel(earlier_ref, start_ref, jump_ref):
    first = lax.axis_index("tm") == 0
    jump_ref[...] = jnp.where(first, 0.0, start_ref[...] - earlier_ref[...])


def sweep_kernel(bricks, slices, tiles_ref, fine_ref, old_ref, *refs):
    coarse_refs = refs[:bricks]
    corrected_ref, change_ref, coef_ref = refs[bricks:]
    own, n = lax.axis_index("space"), lax.axis_index("tm")
    for k in range(bricks):
        coef_ref[(own + bricks - k) % bricks] = coarse_refs[k][...]
    w = [coarse_weights(coef_ref.at[b], b == 0, b == bricks - 1) for b in range(bricks)]

    def coarse_step(m, image):
        c = [image[b] + tiles_ref[b * slices + m] for b in range(bricks)]
        half = [shifted(v, 4, 0) for v in c]
        return tuple(
            coarse_apply(w[b], c[b], half[b], half[max(b - 1, 0)], half[min(b + 1, bricks - 1)])
            for b in range(bricks)
        )

    zero = tuple(jnp.zeros((ROWS, LANES), f32) for _ in range(bricks))
    image = lax.fori_loop(0, n, coarse_step, zero)
    for b in range(bricks):
        change_ref[b] = image[b]
    change = jnp.where(n == 0, 0.0, change_ref[own] - old_ref[...])
    planes = prolong_tile(change)
    for z in range(NZ):
        at = slice(z * ROWS, (z + 1) * ROWS)
        corrected_ref[at] = fine_ref[at] + planes[z // 4]


def local(start_states, velocity, diffusivity):
    bricks, slices = lax.axis_size("space"), lax.axis_size("tm")
    parts = bricks * slices
    ring = lambda count, by: [(i, (i + by) % count) for i in range(count)]
    out = lambda *shape: pltpu.VMEM(shape, f32)
    vmem, anyspace = pl.BlockSpec(memory_space=pltpu.VMEM), pl.BlockSpec(memory_space=pl.ANY)
    inside = lambda *xs: [pltpu.with_memory_space_constraint(x, pltpu.VMEM) for x in xs]

    v, vel, diff, mine_pair, mine_cross = pl.pallas_call(
        edges_kernel,
        in_specs=[anyspace] * 3,
        out_specs=[vmem] * 5,
        out_shape=[
            out(FLAT, LANES),
            out(3 * FLAT, LANES),
            out(FLAT, LANES),
            out(3 * NZ + ROWS, LANES),
            out(3 * NZ + ROWS, LANES),
        ],
        scratch_shapes=[pltpu.SemaphoreType.DMA((3,))],
        name="edges",
    )(
        start_states.reshape(FLAT, LANES),
        velocity.reshape(3 * FLAT, LANES),
        diffusivity.reshape(FLAT, LANES),
    )
    pair = lax.ppermute(mine_pair, "space", [(i, i ^ 1) for i in range(bricks)])
    across = [(i, min(max(((i + 1) ^ 1) - 1, 0), bricks - 1)) for i in range(bricks)]
    cross = lax.ppermute(mine_cross, "space", across)

    q, coarse, keep = pl.pallas_call(
        steps_kernel,
        in_specs=[vmem] * 3,
        out_specs=[vmem] * 3,
        out_shape=[out(FLAT, LANES), out(4, ROWS, LANES), out(12 * NZ, LANES)],
        scratch_shapes=[pltpu.VMEM((FLAT + 2 * ROWS, LANES), f32)] * 2,
        name="steps",
    )(*inside(v, vel, diff))

    fine, tiles, old = pl.pallas_call(
        lambda *refs: finish_kernel(parts, bricks, *refs),
        in_specs=[vmem] * 7,
        out_specs=[vmem] * 3,
        out_shape=[out(FLAT, LANES), out(parts, ROWS, LANES), out(ROWS, LANES)],
        name="finish",
    )(*inside(q, mine_pair, mine_cross, pair, cross, keep, coarse))

    earlier = lax.ppermute(fine, "tm", ring(slices, 1))
    defects = lax.all_to_all(tiles, ("space", "tm"), 0, 0)
    coarse_all = [coarse] + [lax.ppermute(coarse, "space", ring(bricks, k)) for k in range(1, bricks)]

    jump = pl.pallas_call(
        jump_kernel,
        in_specs=[vmem] * 2,
        out_specs=vmem,
        out_shape=jax.ShapeDtypeStruct((FLAT, LANES), f32),
        name="jump",
    )(*inside(earlier, v))
    defects, jump = lax.optimization_barrier((defects, jump))

    corrected = pl.pallas_call(
        lambda *refs: sweep_kernel(bricks, slices, *refs),
        in_specs=[vmem] * (bricks + 3),
        out_specs=vmem,
        out_shape=jax.ShapeDtypeStruct((FLAT, LANES), f32),
        scratch_shapes=[
            pltpu.VMEM((bricks, ROWS, LANES), f32),
            pltpu.VMEM((bricks, 4, ROWS, LANES), f32),
        ],
        name="sweep",
    )(*inside(defects, fine, old, *coarse_all))
    shape = (1, NZ, ROWS, LANES)
    return corrected.reshape(shape), jump.reshape(shape)


def solution(mesh):
    in_specs = (
        P(("groups", "tm"), None, "space", None),
        P(None, None, "space", None),
        P(None, "space", None),
    )
    out_specs = (P(("groups", "tm"), None, "space", None), P(("groups", "tm"), None, "space", None))
    return jax.shard_map(local, mesh=mesh, in_specs=in_specs, out_specs=out_specs, check_vma=False)
```

```python
import jax
import jax.numpy as jnp
from jax import lax
from jax.experimental import pallas as pl
from jax.experimental.pallas import tpu as pltpu
from jax.sharding import PartitionSpec as P

NZ, ROWS, LANES = 64, 8, 128
FLAT = NZ * ROWS
CHUNK = 8
EDGE = 3 * NZ + ROWS
BITS = ((1, 1), (1, 2), (0, 1), (0, 2))

f32 = jnp.float32


def shifted(x, by, axis):
    return pltpu.roll(x, (-by) % x.shape[axis], axis)


def iotas(shape):
    n = len(shape)
    return (
        lax.broadcasted_iota(jnp.int32, shape, n - 2),
        lax.broadcasted_iota(jnp.int32, shape, n - 1),
    )


def restrict_tile(planes):
    sub, lane = iotas((ROWS, LANES))
    for axis, dist in BITS:
        low = ((lane if axis else sub) // dist) % 2 == 0
        planes = [
            jnp.where(low, a + shifted(a, dist, axis), b + shifted(b, -dist, axis))
            for a, b in zip(planes[0::2], planes[1::2])
        ]
    return planes[0]


def prolong_tile(tile):
    sub, lane = iotas((ROWS, LANES))
    planes = [tile]
    for axis, dist in reversed(BITS):
        low = ((lane if axis else sub) // dist) % 2 == 0
        grown = []
        for a in planes:
            grown.append(jnp.where(low, a, shifted(a, -dist, axis)))
            grown.append(jnp.where(low, shifted(a, dist, axis), a))
        planes = grown
    return planes


def plane_sums(ref):
    def one(c):
        at = c * 4 * ROWS
        return (ref[at : at + ROWS] + ref[at + ROWS : at + 2 * ROWS]) + (
            ref[at + 2 * ROWS : at + 3 * ROWS] + ref[at + 3 * ROWS : at + 4 * ROWS]
        )

    return [one(c) for c in range(NZ // 4)]


def weights(cz, cx, cy, diff):
    out = []
    for c in (cz, cx, cy):
        out.append(diff + jnp.maximum(c, 0.0))
        out.append(diff - jnp.minimum(c, 0.0))
    centre = 1.0 - ((out[0] + out[1]) + (out[2] + out[3]) + (out[4] + out[5]))
    return out + [centre]


def row(ref, at):
    return ref[pl.ds(at, NZ, stride=ROWS), :]


def edges_kernel(v_hbm, vel_hbm, d_hbm, v_ref, vel_ref, d_ref, pair_ref, cross_ref, sems):
    copies = [pltpu.make_async_copy(v_hbm, v_ref, sems.at[0])]
    for d in range(3):
        at = pl.ds(d * FLAT, FLAT)
        copies.append(pltpu.make_async_copy(vel_hbm.at[at], vel_ref.at[at], sems.at[1 + d]))
    copies.append(pltpu.make_async_copy(d_hbm, d_ref, sems.at[4]))
    for copy in copies:
        copy.start()
    odd = lax.axis_index("space") % 2 == 1
    fields = (
        (v_ref, 1.0),
        (vel_ref.at[0:FLAT], 0.5),
        (vel_ref.at[FLAT : 2 * FLAT], 0.5),
        (vel_ref.at[2 * FLAT : 3 * FLAT], 0.5),
        (d_ref, 0.125),
    )
    for j, (copy, (ref, factor)) in enumerate(zip(copies, fields)):
        copy.wait()
        tile = restrict_tile(plane_sums(ref)) * (factor / 64)
        pair_ref[3 * NZ + j * ROWS : 3 * NZ + (j + 1) * ROWS] = tile
        if j == 0:
            cross_ref[3 * NZ : EDGE] = tile
    sub, lane = iotas((NZ, LANES))
    rows = []
    for face, inner, side in ((0, 1, 0), (ROWS - 1, ROWS - 2, 1)):
        w = weights(*(row(vel_ref, d * FLAT + face) for d in range(3)), row(d_ref, face))
        v = row(v_ref, face)
        total = w[6] * v + w[3 - side] * row(v_ref, inner)
        total += jnp.where(sub == 0, 0.0, w[0]) * shifted(v, -1, 0)
        total += jnp.where(sub == NZ - 1, 0.0, w[1]) * shifted(v, 1, 0)
        total += jnp.where(lane == 0, 0.0, w[4]) * shifted(v, -1, 1)
        total += jnp.where(lane == LANES - 1, 0.0, w[5]) * shifted(v, 1, 1)
        rows.append((v, total, w[2 + side]))
    for j, (low, high) in enumerate(zip(*rows)):
        pair_ref[j * NZ : (j + 1) * NZ] = jnp.where(odd, low, high)
        cross_ref[j * NZ : (j + 1) * NZ] = jnp.where(odd, high, low)


def steps_kernel(v_ref, vel_ref, d_ref, q_ref, keep_ref, p_ref, pv_ref):
    zero = jnp.zeros((ROWS, LANES), f32)
    for ref in (p_ref, pv_ref):
        ref[0:ROWS] = zero
        ref[FLAT + ROWS : FLAT + 2 * ROWS] = zero
    pv_ref[ROWS : FLAT + ROWS] = v_ref[...]
    shape = (CHUNK, ROWS, LANES)
    sub, lane = iotas(shape)
    size = CHUNK * ROWS

    def step(src, dst, dst_off):
        def body(c, carry):
            at = pl.multiple_of(c * size, size)
            load = lambda ref, off: ref[pl.ds(at + off, size), :].reshape(shape)
            w = weights(
                load(vel_ref, 0), load(vel_ref, FLAT), load(vel_ref, 2 * FLAT), load(d_ref, 0)
            )
            v = load(src, ROWS)
            total = w[6] * v + w[0] * load(src, 0) + w[1] * load(src, 2 * ROWS)
            total += jnp.where(sub == 0, 0.0, w[2]) * shifted(v, -1, 1)
            total += jnp.where(sub == ROWS - 1, 0.0, w[3]) * shifted(v, 1, 1)
            total += jnp.where(lane == 0, 0.0, w[4]) * shifted(v, -1, 2)
            total += jnp.where(lane == LANES - 1, 0.0, w[5]) * shifted(v, 1, 2)
            dst[pl.ds(at + dst_off, size), :] = total.reshape(size, LANES)
            return carry

        lax.fori_loop(0, NZ // CHUNK, body, 0)

    step(pv_ref, p_ref, ROWS)
    step(p_ref, q_ref, 0)
    for side, at in enumerate((0, ROWS - 1)):
        w = weights(*(row(vel_ref, d * FLAT + at) for d in range(3)), row(d_ref, at))
        for j, value in enumerate((w[0], w[1], w[4], w[5], w[6])):
            keep_ref[(side * 6 + j) * NZ : (side * 6 + j + 1) * NZ] = value
    keep_ref[5 * NZ : 6 * NZ] = row(d_ref, 1) + jnp.maximum(row(vel_ref, FLAT + 1), 0.0)
    keep_ref[11 * NZ : 12 * NZ] = row(d_ref, ROWS - 2) - jnp.minimum(row(vel_ref, FLAT + ROWS - 2), 0.0)


def coarse_weights(c, first, last):
    sub, lane = iotas((ROWS, LANES))
    zl, zh, y = lane % 4, sub % 4, lane // 4
    w = weights(c[0], c[1], c[2], c[3])
    w[0] = jnp.where((zl == 0) & (zh == 0), 0.0, w[0])
    w[1] = jnp.where((zl == 3) & (zh == 3), 0.0, w[1])
    w[4] = jnp.where(y == 0, 0.0, w[4])
    w[5] = jnp.where(y == LANES // 4 - 1, 0.0, w[5])
    w[2] = jnp.where((sub < 4) & first, 0.0, w[2])
    w[3] = jnp.where((sub >= 4) & last, 0.0, w[3])
    return w


def coarse_apply(w, v, own, lower, upper):
    sub, lane = iotas((ROWS, LANES))
    zl = lane % 4
    zb = jnp.where(zl == 0, shifted(shifted(v, 3, 1), -1, 0), shifted(v, -1, 1))
    za = jnp.where(zl == 3, shifted(shifted(v, -3, 1), 1, 0), shifted(v, 1, 1))
    xb = jnp.where(sub < 4, lower, own)
    xa = jnp.where(sub < 4, own, upper)
    return (
        (w[6] * v + w[0] * zb + w[1] * za)
        + (w[2] * xb + w[3] * xa)
        + (w[4] * shifted(v, -4, 1) + w[5] * shifted(v, 4, 1))
    )


def finish_kernel(parts, bricks, q_ref, mine_pair_ref, mine_cross_ref, pair_ref, cross_ref, keep_ref, fine_ref, tiles_ref, old_ref, both_ref):
    brick = lax.axis_index("space")
    odd = brick % 2 == 1
    has_low = brick > 0
    has_high = brick < bricks - 1
    part = lambda ref, j: ref[j * NZ : (j + 1) * NZ]

    def sides(pair, cross, j):
        a, b = part(pair, j), part(cross, j)
        return jnp.where(odd, a, b), jnp.where(odd, b, a)

    own = [sides(mine_pair_ref, mine_cross_ref, j) for j in (0, 2)]
    far = [sides(pair_ref, cross_ref, j) for j in range(3)]
    sub, lane = iotas((NZ, LANES))
    fine_ref[...] = q_ref[...]
    for side in range(2):
        wbz, waz, wby, way, centre, inner = (part(keep_ref, side * 6 + j) for j in range(6))
        k = jnp.where(has_high if side else has_low, own[1][side], 0.0)
        delta = k * far[0][side]
        beyond = far[1][side] + far[2][side] * own[0][side]
        edge = centre * delta + k * beyond
        edge += jnp.where(sub == 0, 0.0, wbz) * shifted(delta, -1, 0)
        edge += jnp.where(sub == NZ - 1, 0.0, waz) * shifted(delta, 1, 0)
        edge += jnp.where(lane == 0, 0.0, wby) * shifted(delta, -1, 1)
        edge += jnp.where(lane == LANES - 1, 0.0, way) * shifted(delta, 1, 1)
        e_at, i_at = (0, 1) if side == 0 else (ROWS - 1, ROWS - 2)
        fine_ref[pl.ds(e_at, NZ, stride=ROWS), :] = row(q_ref, e_at) + edge
        fine_ref[pl.ds(i_at, NZ, stride=ROWS), :] = row(q_ref, i_at) + inner * delta
    at = slice(3 * NZ, EDGE)
    v = mine_pair_ref[at]
    lower = jnp.where(odd, pair_ref[at], cross_ref[at])
    upper = jnp.where(odd, cross_ref[at], pair_ref[at])
    mine, other = mine_pair_ref[EDGE:], pair_ref[EDGE:]
    both_ref[0] = jnp.where(odd, other, mine)
    both_ref[1] = jnp.where(odd, mine, other)
    w = coarse_weights(mine.reshape(4, ROWS, LANES), jnp.logical_not(has_low), jnp.logical_not(has_high))
    old = coarse_apply(w, v, *(shifted(x, 4, 0) for x in (v, lower, upper)))
    old_ref[...] = old
    image = restrict_tile(plane_sums(fine_ref)) * (1.0 / 64)
    tile = jnp.where(lax.axis_index("tm") == 0, image, image - old)
    for j in range(parts):
        tiles_ref[j] = tile


def jump_kernel(earlier_ref, start_ref, jump_ref):
    keep = jnp.where(lax.axis_index("tm") == 0, 0.0, 1.0)
    jump_ref[...] = keep * (start_ref[...] - earlier_ref[...])


def sweep_kernel(bricks, slices, tiles_ref, fine_ref, old_ref, *refs):
    coarse_refs = refs[: bricks // 2]
    corrected_ref, change_ref, coef_ref = refs[bricks // 2 :]
    own, n = lax.axis_index("space"), lax.axis_index("tm")
    for k, ref in enumerate(coarse_refs):
        coef_ref[(own // 2 + bricks // 2 - k) % (bricks // 2)] = ref[...]
    w = [
        coarse_weights(coef_ref[b // 2, b % 2].reshape(4, ROWS, LANES), b == 0, b == bricks - 1)
        for b in range(bricks)
    ]

    def coarse_step(m, image):
        c = [image[b] + tiles_ref[b * slices + m] for b in range(bricks)]
        half = [shifted(v, 4, 0) for v in c]
        return tuple(
            coarse_apply(w[b], c[b], half[b], half[max(b - 1, 0)], half[min(b + 1, bricks - 1)])
            for b in range(bricks)
        )

    zero = tuple(jnp.zeros((ROWS, LANES), f32) for _ in range(bricks))
    image = lax.fori_loop(0, n, coarse_step, zero)
    for b in range(bricks):
        change_ref[b] = image[b]
    change = jnp.where(n == 0, 0.0, change_ref[own] - old_ref[...])
    planes = prolong_tile(change)
    for z in range(NZ):
        at = slice(z * ROWS, (z + 1) * ROWS)
        corrected_ref[at] = fine_ref[at] + planes[z // 4]


def local(start_states, velocity, diffusivity):
    bricks, slices = lax.axis_size("space"), lax.axis_size("tm")
    groups, parts = lax.axis_size("groups"), bricks * slices
    ring = lambda count, by: [(i, (i + by) % count) for i in range(count)]
    out = lambda *shape: pltpu.VMEM(shape, f32)
    vmem, anyspace = pl.BlockSpec(memory_space=pltpu.VMEM), pl.BlockSpec(memory_space=pl.ANY)
    inside = lambda *xs: [pltpu.with_memory_space_constraint(x, pltpu.VMEM) for x in xs]

    v, vel, diff, mine_pair, mine_cross = pl.pallas_call(
        edges_kernel,
        in_specs=[anyspace] * 3,
        out_specs=[vmem] * 5,
        out_shape=[
            out(FLAT, LANES),
            out(3 * FLAT, LANES),
            out(FLAT, LANES),
            out(EDGE + 4 * ROWS, LANES),
            out(EDGE, LANES),
        ],
        scratch_shapes=[pltpu.SemaphoreType.DMA((5,))],
        name="edges",
    )(
        start_states.reshape(FLAT, LANES),
        velocity.reshape(3 * FLAT, LANES),
        diffusivity.reshape(FLAT, LANES),
    )
    partner = {}
    for g in range(groups):
        for i in range(bricks):
            j, h = i + 1 if i % 2 else i - 1, g
            if j < 0 or j >= bricks:
                j, h = (i, g ^ 1) if groups % 2 == 0 else (j % bricks, g)
            partner[g * bricks + i] = h * bricks + j
    cross = lax.ppermute(mine_cross, ("groups", "space"), list(partner.items()))

    pair = lax.ppermute(mine_pair, "space", [(i, i ^ 1) for i in range(bricks)])

    q, keep = pl.pallas_call(
        steps_kernel,
        in_specs=[vmem] * 3,
        out_specs=[vmem] * 2,
        out_shape=[out(FLAT, LANES), out(12 * NZ, LANES)],
        scratch_shapes=[pltpu.VMEM((FLAT + 2 * ROWS, LANES), f32)] * 2,
        name="steps",
    )(*inside(v, vel, diff))
    fine, tiles, old, both = pl.pallas_call(
        lambda *refs: finish_kernel(parts, bricks, *refs),
        in_specs=[vmem] * 6,
        out_specs=[vmem] * 4,
        out_shape=[
            out(FLAT, LANES),
            out(parts, ROWS, LANES),
            out(ROWS, LANES),
            out(2, 4 * ROWS, LANES),
        ],
        name="finish",
    )(*inside(q, mine_pair, mine_cross, pair, cross, keep))

    earlier = lax.ppermute(fine, "tm", ring(slices, 1))
    defects = lax.all_to_all(tiles, ("space", "tm"), 0, 0)
    coarse_all = [both] + [
        lax.ppermute(both, "space", ring(bricks, k)) for k in range(2, bricks, 2)
    ]

    jump = pl.pallas_call(
        jump_kernel,
        in_specs=[vmem] * 2,
        out_specs=vmem,
        out_shape=jax.ShapeDtypeStruct((FLAT, LANES), f32),
        name="jump",
    )(*inside(earlier, v))
    defects, jump = lax.optimization_barrier((defects, jump))

    corrected = pl.pallas_call(
        lambda *refs: sweep_kernel(bricks, slices, *refs),
        in_specs=[vmem] * (bricks // 2 + 3),
        out_specs=vmem,
        out_shape=jax.ShapeDtypeStruct((FLAT, LANES), f32),
        scratch_shapes=[
            pltpu.VMEM((bricks, ROWS, LANES), f32),
            pltpu.VMEM((bricks // 2, 2, 4 * ROWS, LANES), f32),
        ],
        name="sweep",
    )(*inside(defects, fine, old, *coarse_all))
    shape = (1, NZ, ROWS, LANES)
    return corrected.reshape(shape), jump.reshape(shape)


def solution(mesh):
    in_specs = (
        P(("groups", "tm"), None, "space", None),
        P(None, None, "space", None),
        P(None, "space", None),
    )
    out_specs = (P(("groups", "tm"), None, "space", None), P(("groups", "tm"), None, "space", None))
    return jax.shard_map(local, mesh=mesh, in_specs=in_specs, out_specs=out_specs, check_vma=False)
```

```python
import jax
import jax.numpy as jnp
from jax import lax
from jax.experimental import pallas as pl
from jax.experimental.pallas import tpu as pltpu
from jax.sharding import PartitionSpec as P

NZ, ROWS, LANES = 64, 8, 128
FLAT = NZ * ROWS
CHUNK = 8
EDGE = 3 * NZ + ROWS
BITS = ((1, 1), (1, 2), (0, 1), (0, 2))

f32 = jnp.float32


def shifted(x, by, axis):
    return pltpu.roll(x, (-by) % x.shape[axis], axis)


def iotas(shape):
    n = len(shape)
    return (
        lax.broadcasted_iota(jnp.int32, shape, n - 2),
        lax.broadcasted_iota(jnp.int32, shape, n - 1),
    )


def restrict_tile(planes):
    sub, lane = iotas((ROWS, LANES))
    for axis, dist in BITS:
        low = ((lane if axis else sub) // dist) % 2 == 0
        planes = [
            jnp.where(low, a + shifted(a, dist, axis), b + shifted(b, -dist, axis))
            for a, b in zip(planes[0::2], planes[1::2])
        ]
    return planes[0]


def prolong_tile(tile):
    sub, lane = iotas((ROWS, LANES))
    planes = [tile]
    for axis, dist in reversed(BITS):
        low = ((lane if axis else sub) // dist) % 2 == 0
        grown = []
        for a in planes:
            grown.append(jnp.where(low, a, shifted(a, -dist, axis)))
            grown.append(jnp.where(low, shifted(a, dist, axis), a))
        planes = grown
    return planes


def plane_sums(ref):
    def one(c):
        at = c * 4 * ROWS
        return (ref[at : at + ROWS] + ref[at + ROWS : at + 2 * ROWS]) + (
            ref[at + 2 * ROWS : at + 3 * ROWS] + ref[at + 3 * ROWS : at + 4 * ROWS]
        )

    return [one(c) for c in range(NZ // 4)]


def weights(cz, cx, cy, diff):
    out = []
    for c in (cz, cx, cy):
        out.append(diff + jnp.maximum(c, 0.0))
        out.append(diff - jnp.minimum(c, 0.0))
    centre = 1.0 - ((out[0] + out[1]) + (out[2] + out[3]) + (out[4] + out[5]))
    return out + [centre]


def row(ref, at):
    return ref[pl.ds(at, NZ, stride=ROWS), :]


def edges_kernel(v_hbm, vel_hbm, d_hbm, v_ref, pair_ref, cross_ref, face_ref, sems):
    copies = [pltpu.make_async_copy(v_hbm, v_ref, sems.at[0])]
    for side, face in enumerate((0, ROWS - 1)):
        for d in range(4):
            src = d_hbm if d == 3 else vel_hbm.at[d]
            j = 4 * side + d
            copies.append(pltpu.make_async_copy(src.at[:, face, :], face_ref.at[j], sems.at[1 + j]))
    for copy in copies:
        copy.start()
    odd = lax.axis_index("space") % 2 == 1
    copies[0].wait()
    image = restrict_tile(plane_sums(v_ref)) * (1.0 / 64)
    for ref in (pair_ref, cross_ref):
        ref[3 * NZ : EDGE] = image
    for copy in copies[1:]:
        copy.wait()
    sub, lane = iotas((NZ, LANES))
    rows = []
    for face, inner, side in ((0, 1, 0), (ROWS - 1, ROWS - 2, 1)):
        w = weights(*(face_ref[4 * side + d] for d in range(4)))
        v = row(v_ref, face)
        total = w[6] * v + w[3 - side] * row(v_ref, inner)
        total += jnp.where(sub == 0, 0.0, w[0]) * shifted(v, -1, 0)
        total += jnp.where(sub == NZ - 1, 0.0, w[1]) * shifted(v, 1, 0)
        total += jnp.where(lane == 0, 0.0, w[4]) * shifted(v, -1, 1)
        total += jnp.where(lane == LANES - 1, 0.0, w[5]) * shifted(v, 1, 1)
        rows.append((v, total, w[2 + side]))
    for j, (low, high) in enumerate(zip(*rows)):
        pair_ref[j * NZ : (j + 1) * NZ] = jnp.where(odd, low, high)
        cross_ref[j * NZ : (j + 1) * NZ] = jnp.where(odd, high, low)


def steps_kernel(v_ref, vel_hbm, d_hbm, q_ref, keep_ref, coarse_ref, p_ref, pv_ref, vel_ref, d_ref, sems):
    copies = [
        pltpu.make_async_copy(src, dst, sems.at[i])
        for i, (src, dst) in enumerate(((d_hbm, d_ref), (vel_hbm, vel_ref)))
    ]
    for copy in copies:
        copy.start()
    zero = jnp.zeros((ROWS, LANES), f32)
    for ref in (p_ref, pv_ref):
        ref[0:ROWS] = zero
        ref[FLAT + ROWS : FLAT + 2 * ROWS] = zero
    pv_ref[ROWS : FLAT + ROWS] = v_ref[...]
    shape = (CHUNK, ROWS, LANES)
    sub, lane = iotas(shape)
    size = CHUNK * ROWS

    def step(src, dst, dst_off):
        def body(c, carry):
            at = pl.multiple_of(c * size, size)
            load = lambda ref, off: ref[pl.ds(at + off, size), :].reshape(shape)
            w = weights(
                load(vel_ref, 0), load(vel_ref, FLAT), load(vel_ref, 2 * FLAT), load(d_ref, 0)
            )
            v = load(src, ROWS)
            total = w[6] * v + w[0] * load(src, 0) + w[1] * load(src, 2 * ROWS)
            total += jnp.where(sub == 0, 0.0, w[2]) * shifted(v, -1, 1)
            total += jnp.where(sub == ROWS - 1, 0.0, w[3]) * shifted(v, 1, 1)
            total += jnp.where(lane == 0, 0.0, w[4]) * shifted(v, -1, 2)
            total += jnp.where(lane == LANES - 1, 0.0, w[5]) * shifted(v, 1, 2)
            dst[pl.ds(at + dst_off, size), :] = total.reshape(size, LANES)
            return carry

        lax.fori_loop(0, NZ // CHUNK, body, 0)

    for copy in copies:
        copy.wait()
    step(pv_ref, p_ref, ROWS)
    step(p_ref, q_ref, 0)
    for side, at in enumerate((0, ROWS - 1)):
        w = weights(*(row(vel_ref, d * FLAT + at) for d in range(3)), row(d_ref, at))
        for j, value in enumerate((w[0], w[1], w[4], w[5], w[6])):
            keep_ref[(side * 6 + j) * NZ : (side * 6 + j + 1) * NZ] = value
    keep_ref[5 * NZ : 6 * NZ] = row(d_ref, 1) + jnp.maximum(row(vel_ref, FLAT + 1), 0.0)
    keep_ref[11 * NZ : 12 * NZ] = row(d_ref, ROWS - 2) - jnp.minimum(row(vel_ref, FLAT + ROWS - 2), 0.0)
    for d in range(3):
        sums = restrict_tile(plane_sums(vel_ref.at[d * FLAT : (d + 1) * FLAT]))
        coarse_ref[d] = sums * (0.5 / 64)
    coarse_ref[3] = restrict_tile(plane_sums(d_ref)) * (0.125 / 64)


def coarse_weights(c, first, last):
    sub, lane = iotas((ROWS, LANES))
    zl, zh, y = lane % 4, sub % 4, lane // 4
    w = weights(c[0], c[1], c[2], c[3])
    w[0] = jnp.where((zl == 0) & (zh == 0), 0.0, w[0])
    w[1] = jnp.where((zl == 3) & (zh == 3), 0.0, w[1])
    w[4] = jnp.where(y == 0, 0.0, w[4])
    w[5] = jnp.where(y == LANES // 4 - 1, 0.0, w[5])
    w[2] = jnp.where((sub < 4) & first, 0.0, w[2])
    w[3] = jnp.where((sub >= 4) & last, 0.0, w[3])
    return w


def coarse_apply(w, v, own, lower, upper):
    sub, lane = iotas((ROWS, LANES))
    zl = lane % 4
    zb = jnp.where(zl == 0, shifted(shifted(v, 3, 1), -1, 0), shifted(v, -1, 1))
    za = jnp.where(zl == 3, shifted(shifted(v, -3, 1), 1, 0), shifted(v, 1, 1))
    xb = jnp.where(sub < 4, lower, own)
    xa = jnp.where(sub < 4, own, upper)
    return (
        (w[6] * v + w[0] * zb + w[1] * za)
        + (w[2] * xb + w[3] * xa)
        + (w[4] * shifted(v, -4, 1) + w[5] * shifted(v, 4, 1))
    )


def finish_kernel(parts, bricks, q_ref, mine_pair_ref, mine_cross_ref, pair_ref, cross_ref, keep_ref, coarse_ref, fine_ref, tiles_ref, old_ref):
    brick = lax.axis_index("space")
    odd = brick % 2 == 1
    has_low = brick > 0
    has_high = brick < bricks - 1
    part = lambda ref, j: ref[j * NZ : (j + 1) * NZ]

    def sides(pair, cross, j):
        a, b = part(pair, j), part(cross, j)
        return jnp.where(odd, a, b), jnp.where(odd, b, a)

    own = [sides(mine_pair_ref, mine_cross_ref, j) for j in (0, 2)]
    far = [sides(pair_ref, cross_ref, j) for j in range(3)]
    sub, lane = iotas((NZ, LANES))
    fine_ref[...] = q_ref[...]
    for side in range(2):
        wbz, waz, wby, way, centre, inner = (part(keep_ref, side * 6 + j) for j in range(6))
        k = jnp.where(has_high if side else has_low, own[1][side], 0.0)
        delta = k * far[0][side]
        beyond = far[1][side] + far[2][side] * own[0][side]
        edge = centre * delta + k * beyond
        edge += jnp.where(sub == 0, 0.0, wbz) * shifted(delta, -1, 0)
        edge += jnp.where(sub == NZ - 1, 0.0, waz) * shifted(delta, 1, 0)
        edge += jnp.where(lane == 0, 0.0, wby) * shifted(delta, -1, 1)
        edge += jnp.where(lane == LANES - 1, 0.0, way) * shifted(delta, 1, 1)
        e_at, i_at = (0, 1) if side == 0 else (ROWS - 1, ROWS - 2)
        fine_ref[pl.ds(e_at, NZ, stride=ROWS), :] = row(q_ref, e_at) + edge
        fine_ref[pl.ds(i_at, NZ, stride=ROWS), :] = row(q_ref, i_at) + inner * delta
    at = slice(3 * NZ, EDGE)
    v = mine_pair_ref[at]
    lower = jnp.where(odd, pair_ref[at], cross_ref[at])
    upper = jnp.where(odd, cross_ref[at], pair_ref[at])
    w = coarse_weights(coarse_ref, jnp.logical_not(has_low), jnp.logical_not(has_high))
    old = coarse_apply(w, v, *(shifted(x, 4, 0) for x in (v, lower, upper)))
    old_ref[...] = old
    image = restrict_tile(plane_sums(fine_ref)) * (1.0 / 64)
    tile = jnp.where(lax.axis_index("tm") == 0, image, image - old)
    for j in range(parts):
        tiles_ref[j] = tile


def jump_kernel(earlier_ref, start_ref, jump_ref):
    keep = jnp.where(lax.axis_index("tm") == 0, 0.0, 1.0)
    jump_ref[...] = keep * (start_ref[...] - earlier_ref[...])


def sweep_kernel(bricks, slices, tiles_ref, fine_ref, old_ref, *refs):
    coarse_refs = refs[:bricks]
    corrected_ref, change_ref, coef_ref = refs[bricks:]
    own, n = lax.axis_index("space"), lax.axis_index("tm")
    for k, ref in enumerate(coarse_refs):
        coef_ref[(own + bricks - k) % bricks] = ref[...]
    w = [
        coarse_weights(coef_ref.at[b], b == 0, b == bricks - 1)
        for b in range(bricks)
    ]

    def coarse_step(m, image):
        c = [image[b] + tiles_ref[b * slices + m] for b in range(bricks)]
        half = [shifted(v, 4, 0) for v in c]
        return tuple(
            coarse_apply(w[b], c[b], half[b], half[max(b - 1, 0)], half[min(b + 1, bricks - 1)])
            for b in range(bricks)
        )

    zero = tuple(jnp.zeros((ROWS, LANES), f32) for _ in range(bricks))
    image = lax.fori_loop(0, n, coarse_step, zero)
    for b in range(bricks):
        change_ref[b] = image[b]
    change = jnp.where(n == 0, 0.0, change_ref[own] - old_ref[...])
    planes = prolong_tile(change)
    for z in range(NZ):
        at = slice(z * ROWS, (z + 1) * ROWS)
        corrected_ref[at] = fine_ref[at] + planes[z // 4]


def local(start_states, velocity, diffusivity):
    bricks, slices = lax.axis_size("space"), lax.axis_size("tm")
    groups, parts = lax.axis_size("groups"), bricks * slices
    ring = lambda count, by: [(i, (i + by) % count) for i in range(count)]
    out = lambda *shape: pltpu.VMEM(shape, f32)
    vmem, anyspace = pl.BlockSpec(memory_space=pltpu.VMEM), pl.BlockSpec(memory_space=pl.ANY)
    inside = lambda *xs: [pltpu.with_memory_space_constraint(x, pltpu.VMEM) for x in xs]

    v, mine_pair, mine_cross = pl.pallas_call(
        edges_kernel,
        in_specs=[anyspace] * 3,
        out_specs=[vmem] * 3,
        out_shape=[
            out(FLAT, LANES),
            out(EDGE, LANES),
            out(EDGE, LANES),
        ],
        scratch_shapes=[pltpu.VMEM((8, NZ, LANES), f32), pltpu.SemaphoreType.DMA((9,))],
        name="edges",
    )(
        start_states.reshape(FLAT, LANES),
        velocity,
        diffusivity,
    )
    partner = {}
    for g in range(groups):
        for i in range(bricks):
            j, h = i + 1 if i % 2 else i - 1, g
            if j < 0 or j >= bricks:
                j, h = (i, g ^ 1) if groups % 2 == 0 else (j % bricks, g)
            partner[g * bricks + i] = h * bricks + j
    cross = lax.ppermute(mine_cross, ("groups", "space"), list(partner.items()))

    pair = lax.ppermute(mine_pair, "space", [(i, i ^ 1) for i in range(bricks)])

    q, keep, coarse = pl.pallas_call(
        steps_kernel,
        in_specs=[vmem, anyspace, anyspace],
        out_specs=[vmem] * 3,
        out_shape=[out(FLAT, LANES), out(12 * NZ, LANES), out(4, ROWS, LANES)],
        scratch_shapes=[pltpu.VMEM((FLAT + 2 * ROWS, LANES), f32)] * 2
        + [
            pltpu.VMEM((3 * FLAT, LANES), f32),
            pltpu.VMEM((FLAT, LANES), f32),
            pltpu.SemaphoreType.DMA((2,)),
        ],
        name="steps",
    )(*inside(v), velocity.reshape(3 * FLAT, LANES), diffusivity.reshape(FLAT, LANES))
    fine, tiles, old = pl.pallas_call(
        lambda *refs: finish_kernel(parts, bricks, *refs),
        in_specs=[vmem] * 7,
        out_specs=[vmem] * 3,
        out_shape=[
            out(FLAT, LANES),
            out(parts, ROWS, LANES),
            out(ROWS, LANES),
        ],
        name="finish",
    )(*inside(q, mine_pair, mine_cross, pair, cross, keep, coarse))

    earlier = lax.ppermute(fine, "tm", ring(slices, 1))
    defects = lax.all_to_all(tiles, ("space", "tm"), 0, 0)
    coarse_all = [coarse] + [
        lax.ppermute(coarse, "space", ring(bricks, k)) for k in range(1, bricks)
    ]

    jump = pl.pallas_call(
        jump_kernel,
        in_specs=[vmem] * 2,
        out_specs=vmem,
        out_shape=jax.ShapeDtypeStruct((FLAT, LANES), f32),
        name="jump",
    )(*inside(earlier, v))
    defects, jump = lax.optimization_barrier((defects, jump))

    corrected = pl.pallas_call(
        lambda *refs: sweep_kernel(bricks, slices, *refs),
        in_specs=[vmem] * (bricks + 3),
        out_specs=vmem,
        out_shape=jax.ShapeDtypeStruct((FLAT, LANES), f32),
        scratch_shapes=[
            pltpu.VMEM((bricks, ROWS, LANES), f32),
            pltpu.VMEM((bricks, 4, ROWS, LANES), f32),
        ],
        name="sweep",
    )(*inside(defects, fine, old, *coarse_all))
    shape = (1, NZ, ROWS, LANES)
    return corrected.reshape(shape), jump.reshape(shape)


def solution(mesh):
    in_specs = (
        P(("groups", "tm"), None, "space", None),
        P(None, None, "space", None),
        P(None, "space", None),
    )
    out_specs = (P(("groups", "tm"), None, "space", None), P(("groups", "tm"), None, "space", None))
    return jax.shard_map(local, mesh=mesh, in_specs=in_specs, out_specs=out_specs, check_vma=False)
```

```python
import jax
import jax.numpy as jnp
from jax import lax
from jax.experimental import pallas as pl
from jax.experimental.pallas import tpu as pltpu
from jax.sharding import PartitionSpec as P

NZ, ROWS, LANES = 64, 8, 128
FLAT = NZ * ROWS
CHUNK = 8
EDGE = 3 * NZ + ROWS
BITS = ((0, 1), (0, 2), (1, 1), (1, 2))

f32 = jnp.float32


def shifted(x, by, axis):
    return pltpu.roll(x, (-by) % x.shape[axis], axis)


def iotas(shape):
    n = len(shape)
    return (
        lax.broadcasted_iota(jnp.int32, shape, n - 2),
        lax.broadcasted_iota(jnp.int32, shape, n - 1),
    )


def restrict_tile(planes):
    sub, lane = iotas((ROWS, LANES))
    for axis, dist in BITS:
        low = ((lane if axis else sub) // dist) % 2 == 0
        planes = [
            jnp.where(low, a + shifted(a, dist, axis), b + shifted(b, -dist, axis))
            for a, b in zip(planes[0::2], planes[1::2])
        ]
    return planes[0]


def prolong_tile(tile):
    sub, lane = iotas((ROWS, LANES))
    planes = [tile]
    for axis, dist in reversed(BITS):
        low = ((lane if axis else sub) // dist) % 2 == 0
        grown = []
        for a in planes:
            grown.append(jnp.where(low, a, shifted(a, -dist, axis)))
            grown.append(jnp.where(low, shifted(a, dist, axis), a))
        planes = grown
    return planes


def plane_sums(ref):
    def one(c):
        at = c * 4 * ROWS
        return (ref[at : at + ROWS] + ref[at + ROWS : at + 2 * ROWS]) + (
            ref[at + 2 * ROWS : at + 3 * ROWS] + ref[at + 3 * ROWS : at + 4 * ROWS]
        )

    return [one(c) for c in range(NZ // 4)]


def weights(cz, cx, cy, diff):
    out = []
    for c in (cz, cx, cy):
        out.append(diff + jnp.maximum(c, 0.0))
        out.append(diff - jnp.minimum(c, 0.0))
    centre = 1.0 - ((out[0] + out[1]) + (out[2] + out[3]) + (out[4] + out[5]))
    return out + [centre]


def row(ref, at):
    return ref[pl.ds(at, NZ, stride=ROWS), :]


def edges_kernel(v_hbm, vel_hbm, d_hbm, v_ref, pair_ref, cross_ref, face_ref, sems):
    copies = [pltpu.make_async_copy(v_hbm, v_ref, sems.at[0])]
    for side, face in enumerate((0, ROWS - 1)):
        for d in range(4):
            src = d_hbm if d == 3 else vel_hbm.at[d]
            j = 4 * side + d
            copies.append(pltpu.make_async_copy(src.at[:, face, :], face_ref.at[j], sems.at[1 + j]))
    for copy in copies:
        copy.start()
    odd = lax.axis_index("space") % 2 == 1
    for copy in copies:
        copy.wait()
    image = restrict_tile(plane_sums(v_ref)) * (1.0 / 64)
    for ref in (pair_ref, cross_ref):
        ref[3 * NZ : EDGE] = image
    sub, lane = iotas((NZ, LANES))
    rows = []
    for face, inner, side in ((0, 1, 0), (ROWS - 1, ROWS - 2, 1)):
        w = weights(*(face_ref[4 * side + d] for d in range(4)))
        v = row(v_ref, face)
        total = w[6] * v + w[3 - side] * row(v_ref, inner)
        total += jnp.where(sub == 0, 0.0, w[0]) * shifted(v, -1, 0)
        total += jnp.where(sub == NZ - 1, 0.0, w[1]) * shifted(v, 1, 0)
        total += jnp.where(lane == 0, 0.0, w[4]) * shifted(v, -1, 1)
        total += jnp.where(lane == LANES - 1, 0.0, w[5]) * shifted(v, 1, 1)
        rows.append((v, total, w[2 + side]))
    for j, (low, high) in enumerate(zip(*rows)):
        pair_ref[j * NZ : (j + 1) * NZ] = jnp.where(odd, low, high)
        cross_ref[j * NZ : (j + 1) * NZ] = jnp.where(odd, high, low)


def steps_kernel(v_ref, vel_hbm, d_hbm, q_ref, keep_ref, coarse_ref, p_ref, pv_ref, vel_ref, d_ref, sems):
    copies = [
        pltpu.make_async_copy(src, dst, sems.at[i])
        for i, (src, dst) in enumerate(((d_hbm, d_ref), (vel_hbm, vel_ref)))
    ]
    for copy in copies:
        copy.start()
    zero = jnp.zeros((ROWS, LANES), f32)
    for ref in (p_ref, pv_ref):
        ref[0:ROWS] = zero
        ref[FLAT + ROWS : FLAT + 2 * ROWS] = zero
    pv_ref[ROWS : FLAT + ROWS] = v_ref[...]
    shape = (CHUNK, ROWS, LANES)
    sub, lane = iotas(shape)
    size = CHUNK * ROWS

    def step(src, dst, dst_off):
        def body(c, carry):
            at = pl.multiple_of(c * size, size)
            load = lambda ref, off: ref[pl.ds(at + off, size), :].reshape(shape)
            w = weights(
                load(vel_ref, 0), load(vel_ref, FLAT), load(vel_ref, 2 * FLAT), load(d_ref, 0)
            )
            v = load(src, ROWS)
            total = w[6] * v + w[0] * load(src, 0) + w[1] * load(src, 2 * ROWS)
            total += jnp.where(sub == 0, 0.0, w[2]) * shifted(v, -1, 1)
            total += jnp.where(sub == ROWS - 1, 0.0, w[3]) * shifted(v, 1, 1)
            total += jnp.where(lane == 0, 0.0, w[4]) * shifted(v, -1, 2)
            total += jnp.where(lane == LANES - 1, 0.0, w[5]) * shifted(v, 1, 2)
            dst[pl.ds(at + dst_off, size), :] = total.reshape(size, LANES)
            return carry

        lax.fori_loop(0, NZ // CHUNK, body, 0)

    for copy in copies:
        copy.wait()
    step(pv_ref, p_ref, ROWS)
    step(p_ref, q_ref, 0)
    for side, at in enumerate((0, ROWS - 1)):
        w = weights(*(row(vel_ref, d * FLAT + at) for d in range(3)), row(d_ref, at))
        for j, value in enumerate((w[0], w[1], w[4], w[5], w[6])):
            keep_ref[(side * 6 + j) * NZ : (side * 6 + j + 1) * NZ] = value
    keep_ref[5 * NZ : 6 * NZ] = row(d_ref, 1) + jnp.maximum(row(vel_ref, FLAT + 1), 0.0)
    keep_ref[11 * NZ : 12 * NZ] = row(d_ref, ROWS - 2) - jnp.minimum(row(vel_ref, FLAT + ROWS - 2), 0.0)
    for d in range(3):
        sums = restrict_tile(plane_sums(vel_ref.at[d * FLAT : (d + 1) * FLAT]))
        coarse_ref[d] = sums * (0.5 / 64)
    coarse_ref[3] = restrict_tile(plane_sums(d_ref)) * (0.125 / 64)


def coarse_weights(c, first, last):
    sub, lane = iotas((ROWS, LANES))
    zl, zh, y = sub % 4, lane % 4, lane // 4
    w = weights(c[0], c[1], c[2], c[3])
    w[0] = jnp.where((zl == 0) & (zh == 0), 0.0, w[0])
    w[1] = jnp.where((zl == 3) & (zh == 3), 0.0, w[1])
    w[4] = jnp.where(y == 0, 0.0, w[4])
    w[5] = jnp.where(y == LANES // 4 - 1, 0.0, w[5])
    w[2] = jnp.where((sub < 4) & first, 0.0, w[2])
    w[3] = jnp.where((sub >= 4) & last, 0.0, w[3])
    return w


def coarse_apply(w, v, own, lower, upper):
    sub, lane = iotas((ROWS, LANES))
    zl = sub % 4
    zb = jnp.where(zl == 0, shifted(shifted(v, -1, 1), 3, 0), shifted(v, -1, 0))
    za = jnp.where(zl == 3, shifted(shifted(v, 1, 1), -3, 0), shifted(v, 1, 0))
    xb = jnp.where(sub < 4, lower, own)
    xa = jnp.where(sub < 4, own, upper)
    return (
        (w[6] * v + w[0] * zb + w[1] * za)
        + (w[2] * xb + w[3] * xa)
        + (w[4] * shifted(v, -4, 1) + w[5] * shifted(v, 4, 1))
    )


def finish_kernel(parts, bricks, q_ref, mine_pair_ref, mine_cross_ref, pair_ref, cross_ref, keep_ref, coarse_ref, fine_ref, tiles_ref, old_ref):
    brick = lax.axis_index("space")
    odd = brick % 2 == 1
    has_low = brick > 0
    has_high = brick < bricks - 1
    part = lambda ref, j: ref[j * NZ : (j + 1) * NZ]

    def sides(pair, cross, j):
        a, b = part(pair, j), part(cross, j)
        return jnp.where(odd, a, b), jnp.where(odd, b, a)

    own = [sides(mine_pair_ref, mine_cross_ref, j) for j in (0, 2)]
    far = [sides(pair_ref, cross_ref, j) for j in range(3)]
    sub, lane = iotas((NZ, LANES))
    fine_ref[...] = q_ref[...]
    for side in range(2):
        wbz, waz, wby, way, centre, inner = (part(keep_ref, side * 6 + j) for j in range(6))
        k = jnp.where(has_high if side else has_low, own[1][side], 0.0)
        delta = k * far[0][side]
        beyond = far[1][side] + far[2][side] * own[0][side]
        edge = centre * delta + k * beyond
        edge += jnp.where(sub == 0, 0.0, wbz) * shifted(delta, -1, 0)
        edge += jnp.where(sub == NZ - 1, 0.0, waz) * shifted(delta, 1, 0)
        edge += jnp.where(lane == 0, 0.0, wby) * shifted(delta, -1, 1)
        edge += jnp.where(lane == LANES - 1, 0.0, way) * shifted(delta, 1, 1)
        e_at, i_at = (0, 1) if side == 0 else (ROWS - 1, ROWS - 2)
        fine_ref[pl.ds(e_at, NZ, stride=ROWS), :] = row(q_ref, e_at) + edge
        fine_ref[pl.ds(i_at, NZ, stride=ROWS), :] = row(q_ref, i_at) + inner * delta
    at = slice(3 * NZ, EDGE)
    v = mine_pair_ref[at]
    lower = jnp.where(odd, pair_ref[at], cross_ref[at])
    upper = jnp.where(odd, cross_ref[at], pair_ref[at])
    w = coarse_weights(coarse_ref, jnp.logical_not(has_low), jnp.logical_not(has_high))
    old = coarse_apply(w, v, *(shifted(x, 4, 0) for x in (v, lower, upper)))
    old_ref[...] = old
    image = restrict_tile(plane_sums(fine_ref)) * (1.0 / 64)
    tile = jnp.where(lax.axis_index("tm") == 0, image, image - old)
    for j in range(parts):
        tiles_ref[j] = tile


def jump_kernel(earlier_ref, start_ref, jump_ref):
    keep = jnp.where(lax.axis_index("tm") == 0, 0.0, 1.0)
    jump_ref[...] = keep * (start_ref[...] - earlier_ref[...])


def sweep_kernel(bricks, slices, tiles_ref, fine_ref, old_ref, *refs):
    coarse_refs = refs[:bricks]
    corrected_ref, change_ref, coef_ref = refs[bricks:]
    own, n = lax.axis_index("space"), lax.axis_index("tm")
    for k, ref in enumerate(coarse_refs):
        coef_ref[(own + bricks - k) % bricks] = ref[...]
    w = [
        coarse_weights(coef_ref.at[b], b == 0, b == bricks - 1)
        for b in range(bricks)
    ]

    def coarse_step(m, image):
        c = [image[b] + tiles_ref[b * slices + m] for b in range(bricks)]
        half = [shifted(v, 4, 0) for v in c]
        return tuple(
            coarse_apply(w[b], c[b], half[b], half[max(b - 1, 0)], half[min(b + 1, bricks - 1)])
            for b in range(bricks)
        )

    zero = tuple(jnp.zeros((ROWS, LANES), f32) for _ in range(bricks))
    image = lax.fori_loop(0, n, coarse_step, zero)
    for b in range(bricks):
        change_ref[b] = image[b]
    change = jnp.where(n == 0, 0.0, change_ref[own] - old_ref[...])
    planes = prolong_tile(change)
    for z in range(NZ):
        at = slice(z * ROWS, (z + 1) * ROWS)
        corrected_ref[at] = fine_ref[at] + planes[z // 4]


def local(start_states, velocity, diffusivity):
    bricks, slices = lax.axis_size("space"), lax.axis_size("tm")
    groups, parts = lax.axis_size("groups"), bricks * slices
    ring = lambda count, by: [(i, (i + by) % count) for i in range(count)]
    out = lambda *shape: pltpu.VMEM(shape, f32)
    vmem, anyspace = pl.BlockSpec(memory_space=pltpu.VMEM), pl.BlockSpec(memory_space=pl.ANY)
    inside = lambda *xs: [pltpu.with_memory_space_constraint(x, pltpu.VMEM) for x in xs]

    v, mine_pair, mine_cross = pl.pallas_call(
        edges_kernel,
        in_specs=[anyspace] * 3,
        out_specs=[vmem] * 3,
        out_shape=[
            out(FLAT, LANES),
            out(EDGE, LANES),
            out(EDGE, LANES),
        ],
        scratch_shapes=[pltpu.VMEM((8, NZ, LANES), f32), pltpu.SemaphoreType.DMA((9,))],
        name="edges",
    )(
        start_states.reshape(FLAT, LANES),
        velocity,
        diffusivity,
    )
    partner = {}
    for g in range(groups):
        for i in range(bricks):
            j, h = i + 1 if i % 2 else i - 1, g
            if j < 0 or j >= bricks:
                j, h = (i, g ^ 1) if groups % 2 == 0 else (j % bricks, g)
            partner[g * bricks + i] = h * bricks + j
    cross = lax.ppermute(mine_cross, ("groups", "space"), list(partner.items()))

    pair = lax.ppermute(mine_pair, "space", [(i, i ^ 1) for i in range(bricks)])

    q, keep, coarse = pl.pallas_call(
        steps_kernel,
        in_specs=[vmem, anyspace, anyspace],
        out_specs=[vmem] * 3,
        out_shape=[out(FLAT, LANES), out(12 * NZ, LANES), out(4, ROWS, LANES)],
        scratch_shapes=[pltpu.VMEM((FLAT + 2 * ROWS, LANES), f32)] * 2
        + [
            pltpu.VMEM((3 * FLAT, LANES), f32),
            pltpu.VMEM((FLAT, LANES), f32),
            pltpu.SemaphoreType.DMA((2,)),
        ],
        name="steps",
    )(*inside(v), velocity.reshape(3 * FLAT, LANES), diffusivity.reshape(FLAT, LANES))
    fine, tiles, old = pl.pallas_call(
        lambda *refs: finish_kernel(parts, bricks, *refs),
        in_specs=[vmem] * 7,
        out_specs=[vmem] * 3,
        out_shape=[
            out(FLAT, LANES),
            out(parts, ROWS, LANES),
            out(ROWS, LANES),
        ],
        name="finish",
    )(*inside(q, mine_pair, mine_cross, pair, cross, keep, coarse))

    earlier = lax.ppermute(fine, "tm", ring(slices, 1))
    defects = lax.all_to_all(tiles, ("space", "tm"), 0, 0)
    coarse_all = [coarse] + [
        lax.ppermute(coarse, "space", ring(bricks, k)) for k in range(1, bricks)
    ]

    jump = pl.pallas_call(
        jump_kernel,
        in_specs=[vmem] * 2,
        out_specs=vmem,
        out_shape=jax.ShapeDtypeStruct((FLAT, LANES), f32),
        name="jump",
    )(*inside(earlier, v))
    defects, jump = lax.optimization_barrier((defects, jump))

    corrected = pl.pallas_call(
        lambda *refs: sweep_kernel(bricks, slices, *refs),
        in_specs=[vmem] * (bricks + 3),
        out_specs=vmem,
        out_shape=jax.ShapeDtypeStruct((FLAT, LANES), f32),
        scratch_shapes=[
            pltpu.VMEM((bricks, ROWS, LANES), f32),
            pltpu.VMEM((bricks, 4, ROWS, LANES), f32),
        ],
        name="sweep",
    )(*inside(defects, fine, old, *coarse_all))
    shape = (1, NZ, ROWS, LANES)
    return corrected.reshape(shape), jump.reshape(shape)


def solution(mesh):
    in_specs = (
        P(("groups", "tm"), None, "space", None),
        P(None, None, "space", None),
        P(None, "space", None),
    )
    out_specs = (P(("groups", "tm"), None, "space", None), P(("groups", "tm"), None, "space", None))
    return jax.shard_map(local, mesh=mesh, in_specs=in_specs, out_specs=out_specs, check_vma=False)
```

```python
import jax
import jax.numpy as jnp
from jax import lax
from jax.experimental import pallas as pl
from jax.experimental.pallas import tpu as pltpu
from jax.sharding import PartitionSpec as P

NZ, ROWS, LANES = 64, 8, 128
FLAT = NZ * ROWS
CHUNK = 8
EDGE = 3 * NZ + ROWS
BITS = ((0, 1), (0, 2), (1, 1), (1, 2))

f32 = jnp.float32


def shifted(x, by, axis):
    return pltpu.roll(x, (-by) % x.shape[axis], axis)


def iotas(shape):
    n = len(shape)
    return (
        lax.broadcasted_iota(jnp.int32, shape, n - 2),
        lax.broadcasted_iota(jnp.int32, shape, n - 1),
    )


def restrict_tile(planes):
    sub, lane = iotas((ROWS, LANES))
    for axis, dist in BITS:
        low = ((lane if axis else sub) // dist) % 2 == 0
        planes = [
            jnp.where(low, a + shifted(a, dist, axis), b + shifted(b, -dist, axis))
            for a, b in zip(planes[0::2], planes[1::2])
        ]
    return planes[0]


def prolong_tile(tile):
    sub, lane = iotas((ROWS, LANES))
    planes = [tile]
    for axis, dist in reversed(BITS):
        low = ((lane if axis else sub) // dist) % 2 == 0
        grown = []
        for a in planes:
            grown.append(jnp.where(low, a, shifted(a, -dist, axis)))
            grown.append(jnp.where(low, shifted(a, dist, axis), a))
        planes = grown
    return planes


def plane_sums(ref):
    def one(c):
        at = c * 4 * ROWS
        return (ref[at : at + ROWS] + ref[at + ROWS : at + 2 * ROWS]) + (
            ref[at + 2 * ROWS : at + 3 * ROWS] + ref[at + 3 * ROWS : at + 4 * ROWS]
        )

    return [one(c) for c in range(NZ // 4)]


def weights(cz, cx, cy, diff):
    out = []
    for c in (cz, cx, cy):
        out.append(diff + jnp.maximum(c, 0.0))
        out.append(diff - jnp.minimum(c, 0.0))
    centre = 1.0 - ((out[0] + out[1]) + (out[2] + out[3]) + (out[4] + out[5]))
    return out + [centre]


def row(ref, at):
    return ref[pl.ds(at, NZ, stride=ROWS), :]


def edges_kernel(v_hbm, vel_hbm, d_hbm, v_ref, pair_ref, cross_ref, face_ref, sems):
    copies = [pltpu.make_async_copy(v_hbm, v_ref, sems.at[0])]
    for side, face in enumerate((0, ROWS - 1)):
        for d in range(4):
            src = d_hbm if d == 3 else vel_hbm.at[d]
            j = 4 * side + d
            copies.append(pltpu.make_async_copy(src.at[:, face, :], face_ref.at[j], sems.at[1 + j]))
    for copy in copies:
        copy.start()
    odd = lax.axis_index("space") % 2 == 1
    for copy in copies:
        copy.wait()
    image = restrict_tile(plane_sums(v_ref)) * (1.0 / 64)
    for ref in (pair_ref, cross_ref):
        ref[3 * NZ : EDGE] = image
    sub, lane = iotas((NZ, LANES))
    rows = []
    for face, inner, side in ((0, 1, 0), (ROWS - 1, ROWS - 2, 1)):
        w = weights(*(face_ref[4 * side + d] for d in range(4)))
        v = row(v_ref, face)
        total = w[6] * v + w[3 - side] * row(v_ref, inner)
        total += jnp.where(sub == 0, 0.0, w[0]) * shifted(v, -1, 0)
        total += jnp.where(sub == NZ - 1, 0.0, w[1]) * shifted(v, 1, 0)
        total += jnp.where(lane == 0, 0.0, w[4]) * shifted(v, -1, 1)
        total += jnp.where(lane == LANES - 1, 0.0, w[5]) * shifted(v, 1, 1)
        rows.append((v, total, w[2 + side]))
    for j, (low, high) in enumerate(zip(*rows)):
        pair_ref[j * NZ : (j + 1) * NZ] = jnp.where(odd, low, high)
        cross_ref[j * NZ : (j + 1) * NZ] = jnp.where(odd, high, low)


def two_steps(v_ref, c_ref, q_ref, p_ref, pv_ref):
    zero = jnp.zeros((ROWS, LANES), f32)
    for ref in (p_ref, pv_ref):
        ref[0:ROWS] = zero
        ref[FLAT + ROWS : FLAT + 2 * ROWS] = zero
    pv_ref[ROWS : FLAT + ROWS] = v_ref[...]
    shape = (CHUNK, ROWS, LANES)
    sub, lane = iotas(shape)
    size = CHUNK * ROWS

    def step(src, dst, dst_off):
        def body(c, carry):
            at = pl.multiple_of(c * size, size)
            load = lambda ref, off: ref[pl.ds(at + off, size), :].reshape(shape)
            w = weights(*(load(c_ref, d * FLAT) for d in range(4)))
            v = load(src, ROWS)
            total = w[6] * v + w[0] * load(src, 0) + w[1] * load(src, 2 * ROWS)
            total += jnp.where(sub == 0, 0.0, w[2]) * shifted(v, -1, 1)
            total += jnp.where(sub == ROWS - 1, 0.0, w[3]) * shifted(v, 1, 1)
            total += jnp.where(lane == 0, 0.0, w[4]) * shifted(v, -1, 2)
            total += jnp.where(lane == LANES - 1, 0.0, w[5]) * shifted(v, 1, 2)
            dst[pl.ds(at + dst_off, size), :] = total.reshape(size, LANES)
            return carry

        lax.fori_loop(0, NZ // CHUNK, body, 0)

    step(pv_ref, p_ref, ROWS)
    step(p_ref, q_ref, 0)


def steps_kernel(v_ref, vel_hbm, d_hbm, q_ref, keep_ref, coarse_ref, c_ref, p_ref, pv_ref, sems):
    parts = ((d_hbm, pl.ds(3 * FLAT, FLAT)), (vel_hbm, pl.ds(0, 3 * FLAT)))
    copies = [
        pltpu.make_async_copy(src, c_ref.at[at], sems.at[i]) for i, (src, at) in enumerate(parts)
    ]
    for copy in copies:
        copy.start()
    for copy in copies:
        copy.wait()
    two_steps(v_ref, c_ref, q_ref, p_ref, pv_ref)
    for side, at in enumerate((0, ROWS - 1)):
        w = weights(*(row(c_ref, d * FLAT + at) for d in range(4)))
        for j, value in enumerate((w[0], w[1], w[4], w[5], w[6])):
            keep_ref[(side * 6 + j) * NZ : (side * 6 + j + 1) * NZ] = value
    keep_ref[5 * NZ : 6 * NZ] = row(c_ref, 3 * FLAT + 1) + jnp.maximum(row(c_ref, FLAT + 1), 0.0)
    keep_ref[11 * NZ : 12 * NZ] = row(c_ref, 3 * FLAT + ROWS - 2) - jnp.minimum(row(c_ref, FLAT + ROWS - 2), 0.0)
    for d, factor in enumerate((0.5, 0.5, 0.5, 0.125)):
        sums = restrict_tile(plane_sums(c_ref.at[d * FLAT : (d + 1) * FLAT]))
        coarse_ref[d] = sums * (factor / 64)


def coarse_weights(c, first, last):
    sub, lane = iotas((ROWS, LANES))
    zl, zh, y = sub % 4, lane % 4, lane // 4
    w = weights(c[0], c[1], c[2], c[3])
    w[0] = jnp.where((zl == 0) & (zh == 0), 0.0, w[0])
    w[1] = jnp.where((zl == 3) & (zh == 3), 0.0, w[1])
    w[4] = jnp.where(y == 0, 0.0, w[4])
    w[5] = jnp.where(y == LANES // 4 - 1, 0.0, w[5])
    w[2] = jnp.where((sub < 4) & first, 0.0, w[2])
    w[3] = jnp.where((sub >= 4) & last, 0.0, w[3])
    return w


def coarse_apply(w, v, own, lower, upper):
    sub, lane = iotas((ROWS, LANES))
    zl = sub % 4
    zb = jnp.where(zl == 0, shifted(shifted(v, -1, 1), 3, 0), shifted(v, -1, 0))
    za = jnp.where(zl == 3, shifted(shifted(v, 1, 1), -3, 0), shifted(v, 1, 0))
    xb = jnp.where(sub < 4, lower, own)
    xa = jnp.where(sub < 4, own, upper)
    return (
        (w[6] * v + w[0] * zb + w[1] * za)
        + (w[2] * xb + w[3] * xa)
        + (w[4] * shifted(v, -4, 1) + w[5] * shifted(v, 4, 1))
    )


def finish_kernel(bricks, q_ref, mine_pair_ref, mine_cross_ref, pair_ref, cross_ref, keep_ref, coarse_ref, fine_ref, message_ref, old_ref, added_ref):
    brick = lax.axis_index("space")
    odd = brick % 2 == 1
    has_low = brick > 0
    has_high = brick < bricks - 1
    part = lambda ref, j: ref[j * NZ : (j + 1) * NZ]

    def sides(pair, cross, j):
        a, b = part(pair, j), part(cross, j)
        return jnp.where(odd, a, b), jnp.where(odd, b, a)

    own = [sides(mine_pair_ref, mine_cross_ref, j) for j in (0, 2)]
    far = [sides(pair_ref, cross_ref, j) for j in range(3)]
    sub, lane = iotas((NZ, LANES))
    fine_ref[...] = q_ref[...]
    for side in range(2):
        wbz, waz, wby, way, centre, inner = (part(keep_ref, side * 6 + j) for j in range(6))
        k = jnp.where(has_high if side else has_low, own[1][side], 0.0)
        delta = k * far[0][side]
        beyond = far[1][side] + far[2][side] * own[0][side]
        edge = centre * delta + k * beyond
        edge += jnp.where(sub == 0, 0.0, wbz) * shifted(delta, -1, 0)
        edge += jnp.where(sub == NZ - 1, 0.0, waz) * shifted(delta, 1, 0)
        edge += jnp.where(lane == 0, 0.0, wby) * shifted(delta, -1, 1)
        edge += jnp.where(lane == LANES - 1, 0.0, way) * shifted(delta, 1, 1)
        e_at, i_at = (0, 1) if side == 0 else (ROWS - 1, ROWS - 2)
        for j, (at, extra) in enumerate(((e_at, edge), (i_at, inner * delta))):
            fine_ref[pl.ds(at, NZ, stride=ROWS), :] = row(q_ref, at) + extra
            added_ref[(2 * side + j) * NZ : (2 * side + j + 1) * NZ] = extra
    at = slice(3 * NZ, EDGE)
    v = mine_pair_ref[at]
    lower = jnp.where(odd, pair_ref[at], cross_ref[at])
    upper = jnp.where(odd, cross_ref[at], pair_ref[at])
    w = coarse_weights(coarse_ref, jnp.logical_not(has_low), jnp.logical_not(has_high))
    old = coarse_apply(w, v, *(shifted(x, 4, 0) for x in (v, lower, upper)))
    old_ref[...] = old
    image = restrict_tile(plane_sums(fine_ref)) * (1.0 / 64)
    message_ref[0] = jnp.where(lax.axis_index("tm") == 0, image, image - old)
    message_ref[1:5] = coarse_ref[...]


def sweep_kernel(bricks, slices, message_ref, partner_ref, got_ref, swapped_ref, fine_ref, old_ref, earlier_ref, added_ref, start_ref, corrected_ref, jump_ref, change_ref, tiles_ref, coef_ref):
    own, n = lax.axis_index("space"), lax.axis_index("tm")
    chips, chip, core = bricks // 2, own // 2, own % 2
    coef_ref[own] = message_ref[1:5]
    coef_ref[2 * chip + 1 - core] = partner_ref[1:5]
    for ref, c in ((got_ref, core), (swapped_ref, 1 - core)):
        at = 0
        for group in range(pl.cdiv(chips, 2)):
            source = (chip + 2 * chips - 2 * group - c) % chips
            for k in range(1, slices):
                for j in range(2):
                    brick = 2 * source + (c if j == 0 else 1 - c)
                    tiles_ref[k, brick] = ref[at]
                    if k == 1:
                        coef_ref[brick] = ref[at + 1 : at + 5]
                    at += 5 if k == 1 else 1
    w = [
        coarse_weights(coef_ref.at[b], b == 0, b == bricks - 1)
        for b in range(bricks)
    ]

    def coarse_step(m, image):
        c = [image[b] + tiles_ref[n - m, b] for b in range(bricks)]
        half = [shifted(v, 4, 0) for v in c]
        return tuple(
            coarse_apply(w[b], c[b], half[b], half[max(b - 1, 0)], half[min(b + 1, bricks - 1)])
            for b in range(bricks)
        )

    zero = tuple(jnp.zeros((ROWS, LANES), f32) for _ in range(bricks))
    image = lax.fori_loop(0, n, coarse_step, zero)
    for b in range(bricks):
        change_ref[b] = image[b]
    change = jnp.where(n == 0, 0.0, change_ref[own] - old_ref[...])
    planes = prolong_tile(change)
    for z in range(NZ):
        at = slice(z * ROWS, (z + 1) * ROWS)
        corrected_ref[at] = fine_ref[at] + planes[z // 4]
    keep = jnp.where(n == 0, 0.0, 1.0)
    jump_ref[...] = keep * (start_ref[...] - earlier_ref[...])
    for j, at in enumerate((0, 1, ROWS - 1, ROWS - 2)):
        extra = added_ref[j * NZ : (j + 1) * NZ]
        jump_ref[pl.ds(at, NZ, stride=ROWS), :] = row(jump_ref, at) - keep * extra


def local(start_states, velocity, diffusivity):
    bricks, slices = lax.axis_size("space"), lax.axis_size("tm")
    groups = lax.axis_size("groups")
    ring = lambda count, by: [(i, (i + by) % count) for i in range(count)]
    out = lambda *shape: pltpu.VMEM(shape, f32)
    vmem, anyspace = pl.BlockSpec(memory_space=pltpu.VMEM), pl.BlockSpec(memory_space=pl.ANY)
    inside = lambda *xs: [pltpu.with_memory_space_constraint(x, pltpu.VMEM) for x in xs]

    v, mine_pair, mine_cross = pl.pallas_call(
        edges_kernel,
        in_specs=[anyspace] * 3,
        out_specs=[vmem] * 3,
        out_shape=[
            out(FLAT, LANES),
            out(EDGE, LANES),
            out(EDGE, LANES),
        ],
        scratch_shapes=[pltpu.VMEM((8, NZ, LANES), f32), pltpu.SemaphoreType.DMA((9,))],
        name="edges",
    )(
        start_states.reshape(FLAT, LANES),
        velocity,
        diffusivity,
    )
    partner = {}
    for g in range(groups):
        for i in range(bricks):
            j, h = i + 1 if i % 2 else i - 1, g
            if j < 0 or j >= bricks:
                j, h = (i, g ^ 1) if groups % 2 == 0 else (j % bricks, g)
            partner[g * bricks + i] = h * bricks + j
    cross = lax.ppermute(mine_cross, ("groups", "space"), list(partner.items()))

    pair = lax.ppermute(mine_pair, "space", [(i, i ^ 1) for i in range(bricks)])

    start_before = lax.ppermute(v, "tm", ring(slices, 1))

    q, keep, coarse, fields = pl.pallas_call(
        steps_kernel,
        in_specs=[vmem, anyspace, anyspace],
        out_specs=[vmem] * 4,
        out_shape=[
            out(FLAT, LANES),
            out(12 * NZ, LANES),
            out(4, ROWS, LANES),
            out(4 * FLAT, LANES),
        ],
        scratch_shapes=[pltpu.VMEM((FLAT + 2 * ROWS, LANES), f32)] * 2
        + [pltpu.SemaphoreType.DMA((2,))],
        name="steps",
    )(*inside(v), velocity.reshape(3 * FLAT, LANES), diffusivity.reshape(FLAT, LANES))
    fine, message, old, added = pl.pallas_call(
        lambda *refs: finish_kernel(bricks, *refs),
        in_specs=[vmem] * 7,
        out_specs=[vmem] * 4,
        out_shape=[
            out(FLAT, LANES),
            out(5, ROWS, LANES),
            out(ROWS, LANES),
            out(4 * NZ, LANES),
        ],
        name="finish",
    )(*inside(q, mine_pair, mine_cross, pair, cross, keep, coarse))

    chips = bricks // 2
    swap = [(i, i ^ 1) for i in range(bricks)]

    def send(value, group, k):
        pairs = []
        for i in range(bricks):
            to = 2 * ((i // 2 + 2 * group + i % 2) % chips) + i % 2
            pairs += [(i * slices + t, to * slices + (t + k) % slices) for t in range(slices)]
        return lax.ppermute(value, ("space", "tm"), pairs)

    partner = lax.ppermute(message, "space", swap)
    added = lax.ppermute(added, "tm", ring(slices, 1))
    earlier = pl.pallas_call(
        two_steps,
        in_specs=[vmem] * 2,
        out_specs=vmem,
        out_shape=out(FLAT, LANES),
        scratch_shapes=[pltpu.VMEM((FLAT + 2 * ROWS, LANES), f32)] * 2,
        name="steps_before",
    )(*inside(start_before, fields))
    both = jnp.concatenate([message, partner])
    tiles = jnp.stack([message[0], partner[0]])
    got = [
        send(both if k == 1 else tiles, group, k)
        for group in range(pl.cdiv(chips, 2))
        for k in range(1, slices)
    ]
    got[0], earlier = lax.optimization_barrier((got[0], earlier))
    got = jnp.concatenate(got)
    swapped = lax.ppermute(got, "space", swap)

    corrected, jump = pl.pallas_call(
        lambda *refs: sweep_kernel(bricks, slices, *refs),
        in_specs=[vmem] * 9,
        out_specs=[vmem] * 2,
        out_shape=[jax.ShapeDtypeStruct((FLAT, LANES), f32)] * 2,
        scratch_shapes=[
            pltpu.VMEM((bricks, ROWS, LANES), f32),
            pltpu.VMEM((slices, bricks, ROWS, LANES), f32),
            pltpu.VMEM((bricks, 4, ROWS, LANES), f32),
        ],
        name="sweep",
    )(*inside(message, partner, got, swapped, fine, old, earlier, added, v))
    shape = (1, NZ, ROWS, LANES)
    return corrected.reshape(shape), jump.reshape(shape)


def solution(mesh):
    in_specs = (
        P(("groups", "tm"), None, "space", None),
        P(None, None, "space", None),
        P(None, "space", None),
    )
    out_specs = (P(("groups", "tm"), None, "space", None), P(("groups", "tm"), None, "space", None))
    return jax.shard_map(local, mesh=mesh, in_specs=in_specs, out_specs=out_specs, check_vma=False)
```

```python
import jax
import jax.numpy as jnp
from jax import lax
from jax.experimental import pallas as pl
from jax.experimental.pallas import tpu as pltpu
from jax.sharding import PartitionSpec as P

NZ, ROWS, LANES = 64, 8, 128
FLAT = NZ * ROWS
CHUNK = 8
EDGE = 3 * NZ + ROWS
BITS = ((0, 1), (0, 2), (1, 1), (1, 2))

f32 = jnp.float32


def shifted(x, by, axis):
    return pltpu.roll(x, (-by) % x.shape[axis], axis)


def iotas(shape):
    n = len(shape)
    return (
        lax.broadcasted_iota(jnp.int32, shape, n - 2),
        lax.broadcasted_iota(jnp.int32, shape, n - 1),
    )


def restrict_tile(planes):
    sub, lane = iotas((ROWS, LANES))
    for axis, dist in BITS:
        low = ((lane if axis else sub) // dist) % 2 == 0
        planes = [
            jnp.where(low, a + shifted(a, dist, axis), b + shifted(b, -dist, axis))
            for a, b in zip(planes[0::2], planes[1::2])
        ]
    return planes[0]


def prolong_tile(tile):
    sub, lane = iotas((ROWS, LANES))
    planes = [tile]
    for axis, dist in reversed(BITS):
        low = ((lane if axis else sub) // dist) % 2 == 0
        grown = []
        for a in planes:
            grown.append(jnp.where(low, a, shifted(a, -dist, axis)))
            grown.append(jnp.where(low, shifted(a, dist, axis), a))
        planes = grown
    return planes


def plane_sums(ref):
    def one(c):
        at = c * 4 * ROWS
        return (ref[at : at + ROWS] + ref[at + ROWS : at + 2 * ROWS]) + (
            ref[at + 2 * ROWS : at + 3 * ROWS] + ref[at + 3 * ROWS : at + 4 * ROWS]
        )

    return [one(c) for c in range(NZ // 4)]


def weights(cz, cx, cy, diff):
    out = []
    for c in (cz, cx, cy):
        out.append(diff + jnp.maximum(c, 0.0))
        out.append(diff - jnp.minimum(c, 0.0))
    centre = 1.0 - ((out[0] + out[1]) + (out[2] + out[3]) + (out[4] + out[5]))
    return out + [centre]


def row(ref, at):
    return ref[pl.ds(at, NZ, stride=ROWS), :]


def edges_kernel(v_hbm, vel_hbm, d_hbm, v_ref, pair_ref, cross_ref, face_ref, sems):
    copies = [pltpu.make_async_copy(v_hbm, v_ref, sems.at[0])]
    for side, face in enumerate((0, ROWS - 1)):
        for d in range(4):
            src = d_hbm if d == 3 else vel_hbm.at[d]
            j = 4 * side + d
            copies.append(pltpu.make_async_copy(src.at[:, face, :], face_ref.at[j], sems.at[1 + j]))
    for copy in copies:
        copy.start()
    odd = lax.axis_index("space") % 2 == 1
    for copy in copies:
        copy.wait()
    image = restrict_tile(plane_sums(v_ref)) * (1.0 / 64)
    for ref in (pair_ref, cross_ref):
        ref[3 * NZ : EDGE] = image
    sub, lane = iotas((NZ, LANES))
    rows = []
    for face, inner, side in ((0, 1, 0), (ROWS - 1, ROWS - 2, 1)):
        w = weights(*(face_ref[4 * side + d] for d in range(4)))
        v = row(v_ref, face)
        total = w[6] * v + w[3 - side] * row(v_ref, inner)
        total += jnp.where(sub == 0, 0.0, w[0]) * shifted(v, -1, 0)
        total += jnp.where(sub == NZ - 1, 0.0, w[1]) * shifted(v, 1, 0)
        total += jnp.where(lane == 0, 0.0, w[4]) * shifted(v, -1, 1)
        total += jnp.where(lane == LANES - 1, 0.0, w[5]) * shifted(v, 1, 1)
        rows.append((v, total, w[2 + side]))
    for j, (low, high) in enumerate(zip(*rows)):
        pair_ref[j * NZ : (j + 1) * NZ] = jnp.where(odd, low, high)
        cross_ref[j * NZ : (j + 1) * NZ] = jnp.where(odd, high, low)


def two_steps(v_ref, c_ref, q_ref, p_ref, pv_ref, waits=()):
    zero = jnp.zeros((ROWS, LANES), f32)
    for ref in (p_ref, pv_ref):
        ref[0:ROWS] = zero
        ref[FLAT + ROWS : FLAT + 2 * ROWS] = zero
    pv_ref[ROWS : FLAT + ROWS] = v_ref[...]
    shape = (CHUNK, ROWS, LANES)
    sub, lane = iotas(shape)
    size = CHUNK * ROWS

    def step(src, dst, dst_off):
        def body(c, carry):
            at = pl.multiple_of(c * size, size)
            load = lambda ref, off: ref[pl.ds(at + off, size), :].reshape(shape)
            w = weights(*(load(c_ref, d * FLAT) for d in range(4)))
            v = load(src, ROWS)
            total = w[6] * v + w[0] * load(src, 0) + w[1] * load(src, 2 * ROWS)
            total += jnp.where(sub == 0, 0.0, w[2]) * shifted(v, -1, 1)
            total += jnp.where(sub == ROWS - 1, 0.0, w[3]) * shifted(v, 1, 1)
            total += jnp.where(lane == 0, 0.0, w[4]) * shifted(v, -1, 2)
            total += jnp.where(lane == LANES - 1, 0.0, w[5]) * shifted(v, 1, 2)
            dst[pl.ds(at + dst_off, size), :] = total.reshape(size, LANES)
            return carry

        return lambda first, last: lax.fori_loop(first, last, body, 0)

    chunks = NZ // CHUNK
    first_step = step(pv_ref, p_ref, ROWS)
    for half, copies in enumerate(waits or ((), ())):
        for copy in copies:
            copy.wait()
        first_step(half * chunks // 2, (half + 1) * chunks // 2)
    step(p_ref, q_ref, 0)(0, chunks)


def steps_kernel(v_ref, vel_hbm, d_hbm, q_ref, keep_ref, coarse_ref, c_ref, p_ref, pv_ref, sems):
    copies = []
    for half in range(2):
        for d in range(4):
            src, at = (vel_hbm, d * FLAT) if d < 3 else (d_hbm, 0)
            at, to = at + half * FLAT // 2, d * FLAT + half * FLAT // 2
            copies.append(
                pltpu.make_async_copy(
                    src.at[pl.ds(at, FLAT // 2)], c_ref.at[pl.ds(to, FLAT // 2)], sems.at[4 * half + d]
                )
            )
    for copy in copies:
        copy.start()
    two_steps(v_ref, c_ref, q_ref, p_ref, pv_ref, (copies[:4], copies[4:]))
    for side, at in enumerate((0, ROWS - 1)):
        w = weights(*(row(c_ref, d * FLAT + at) for d in range(4)))
        for j, value in enumerate((w[0], w[1], w[4], w[5], w[6])):
            keep_ref[(side * 6 + j) * NZ : (side * 6 + j + 1) * NZ] = value
    keep_ref[5 * NZ : 6 * NZ] = row(c_ref, 3 * FLAT + 1) + jnp.maximum(row(c_ref, FLAT + 1), 0.0)
    keep_ref[11 * NZ : 12 * NZ] = row(c_ref, 3 * FLAT + ROWS - 2) - jnp.minimum(row(c_ref, FLAT + ROWS - 2), 0.0)
    for d, factor in enumerate((0.5, 0.5, 0.5, 0.125)):
        sums = restrict_tile(plane_sums(c_ref.at[d * FLAT : (d + 1) * FLAT]))
        coarse_ref[d] = sums * (factor / 64)


def coarse_weights(c, first, last):
    sub, lane = iotas((ROWS, LANES))
    zl, zh, y = sub % 4, lane % 4, lane // 4
    w = weights(c[0], c[1], c[2], c[3])
    w[0] = jnp.where((zl == 0) & (zh == 0), 0.0, w[0])
    w[1] = jnp.where((zl == 3) & (zh == 3), 0.0, w[1])
    w[4] = jnp.where(y == 0, 0.0, w[4])
    w[5] = jnp.where(y == LANES // 4 - 1, 0.0, w[5])
    w[2] = jnp.where((sub < 4) & first, 0.0, w[2])
    w[3] = jnp.where((sub >= 4) & last, 0.0, w[3])
    return w


def coarse_apply(w, v, own, lower, upper):
    sub, lane = iotas((ROWS, LANES))
    zl = sub % 4
    zb = jnp.where(zl == 0, shifted(shifted(v, -1, 1), 3, 0), shifted(v, -1, 0))
    za = jnp.where(zl == 3, shifted(shifted(v, 1, 1), -3, 0), shifted(v, 1, 0))
    xb = jnp.where(sub < 4, lower, own)
    xa = jnp.where(sub < 4, own, upper)
    return (
        (w[6] * v + w[0] * zb + w[1] * za)
        + (w[2] * xb + w[3] * xa)
        + (w[4] * shifted(v, -4, 1) + w[5] * shifted(v, 4, 1))
    )


def finish_kernel(bricks, q_ref, mine_pair_ref, mine_cross_ref, pair_ref, cross_ref, keep_ref, coarse_ref, fine_ref, message_ref, old_ref, added_ref):
    brick = lax.axis_index("space")
    odd = brick % 2 == 1
    has_low = brick > 0
    has_high = brick < bricks - 1
    part = lambda ref, j: ref[j * NZ : (j + 1) * NZ]

    def sides(pair, cross, j):
        a, b = part(pair, j), part(cross, j)
        return jnp.where(odd, a, b), jnp.where(odd, b, a)

    own = [sides(mine_pair_ref, mine_cross_ref, j) for j in (0, 2)]
    far = [sides(pair_ref, cross_ref, j) for j in range(3)]
    sub, lane = iotas((NZ, LANES))
    fine_ref[...] = q_ref[...]
    for side in range(2):
        wbz, waz, wby, way, centre, inner = (part(keep_ref, side * 6 + j) for j in range(6))
        k = jnp.where(has_high if side else has_low, own[1][side], 0.0)
        delta = k * far[0][side]
        beyond = far[1][side] + far[2][side] * own[0][side]
        edge = centre * delta + k * beyond
        edge += jnp.where(sub == 0, 0.0, wbz) * shifted(delta, -1, 0)
        edge += jnp.where(sub == NZ - 1, 0.0, waz) * shifted(delta, 1, 0)
        edge += jnp.where(lane == 0, 0.0, wby) * shifted(delta, -1, 1)
        edge += jnp.where(lane == LANES - 1, 0.0, way) * shifted(delta, 1, 1)
        e_at, i_at = (0, 1) if side == 0 else (ROWS - 1, ROWS - 2)
        for j, (at, extra) in enumerate(((e_at, edge), (i_at, inner * delta))):
            fine_ref[pl.ds(at, NZ, stride=ROWS), :] = row(q_ref, at) + extra
            added_ref[(2 * side + j) * NZ : (2 * side + j + 1) * NZ] = extra
    at = slice(3 * NZ, EDGE)
    v = mine_pair_ref[at]
    lower = jnp.where(odd, pair_ref[at], cross_ref[at])
    upper = jnp.where(odd, cross_ref[at], pair_ref[at])
    w = coarse_weights(coarse_ref, jnp.logical_not(has_low), jnp.logical_not(has_high))
    old = coarse_apply(w, v, *(shifted(x, 4, 0) for x in (v, lower, upper)))
    old_ref[...] = old
    image = restrict_tile(plane_sums(fine_ref)) * (1.0 / 64)
    message_ref[0] = jnp.where(lax.axis_index("tm") == 0, image, image - old)
    message_ref[1:5] = coarse_ref[...]


def sweep_kernel(bricks, slices, message_ref, partner_ref, got_ref, swapped_ref, fine_ref, old_ref, earlier_ref, added_ref, start_ref, corrected_ref, jump_ref, change_ref, tiles_ref, coef_ref):
    own, n = lax.axis_index("space"), lax.axis_index("tm")
    chips, chip, core = bricks // 2, own // 2, own % 2
    coef_ref[own] = message_ref[1:5]
    coef_ref[2 * chip + 1 - core] = partner_ref[1:5]
    for ref, c in ((got_ref, core), (swapped_ref, 1 - core)):
        at = 0
        for group in range(pl.cdiv(chips, 2)):
            source = (chip + 2 * chips - 2 * group - c) % chips
            for k in range(1, slices):
                for j in range(2):
                    brick = 2 * source + (c if j == 0 else 1 - c)
                    tiles_ref[k, brick] = ref[at]
                    if k == slices - 1:
                        coef_ref[brick] = ref[at + 1 : at + 5]
                    at += 5 if k == slices - 1 else 1
    w = [
        coarse_weights(coef_ref.at[b], b == 0, b == bricks - 1)
        for b in range(bricks)
    ]

    def coarse_step(m, image):
        c = [image[b] + tiles_ref[n - m, b] for b in range(bricks)]
        half = [shifted(v, 4, 0) for v in c]
        return tuple(
            coarse_apply(w[b], c[b], half[b], half[max(b - 1, 0)], half[min(b + 1, bricks - 1)])
            for b in range(bricks)
        )

    zero = tuple(jnp.zeros((ROWS, LANES), f32) for _ in range(bricks))
    image = lax.fori_loop(0, n, coarse_step, zero)
    for b in range(bricks):
        change_ref[b] = image[b]
    change = jnp.where(n == 0, 0.0, change_ref[own] - old_ref[...])
    planes = prolong_tile(change)
    for z in range(NZ):
        at = slice(z * ROWS, (z + 1) * ROWS)
        corrected_ref[at] = fine_ref[at] + planes[z // 4]
    keep = jnp.where(n == 0, 0.0, 1.0)
    jump_ref[...] = keep * (start_ref[...] - earlier_ref[...])
    for j, at in enumerate((0, 1, ROWS - 1, ROWS - 2)):
        extra = added_ref[j * NZ : (j + 1) * NZ]
        jump_ref[pl.ds(at, NZ, stride=ROWS), :] = row(jump_ref, at) - keep * extra


def local(start_states, velocity, diffusivity):
    bricks, slices = lax.axis_size("space"), lax.axis_size("tm")
    groups = lax.axis_size("groups")
    ring = lambda count, by: [(i, (i + by) % count) for i in range(count)]
    out = lambda *shape: pltpu.VMEM(shape, f32)
    vmem, anyspace = pl.BlockSpec(memory_space=pltpu.VMEM), pl.BlockSpec(memory_space=pl.ANY)
    inside = lambda *xs: [pltpu.with_memory_space_constraint(x, pltpu.VMEM) for x in xs]

    v, mine_pair, mine_cross = pl.pallas_call(
        edges_kernel,
        in_specs=[anyspace] * 3,
        out_specs=[vmem] * 3,
        out_shape=[
            out(FLAT, LANES),
            out(EDGE, LANES),
            out(EDGE, LANES),
        ],
        scratch_shapes=[pltpu.VMEM((8, NZ, LANES), f32), pltpu.SemaphoreType.DMA((9,))],
        name="edges",
    )(
        start_states.reshape(FLAT, LANES),
        velocity,
        diffusivity,
    )
    partner = {}
    for g in range(groups):
        for i in range(bricks):
            j, h = i + 1 if i % 2 else i - 1, g
            if j < 0 or j >= bricks:
                j, h = (i, g ^ 1) if groups % 2 == 0 else (j % bricks, g)
            partner[g * bricks + i] = h * bricks + j
    cross = lax.ppermute(mine_cross, ("groups", "space"), list(partner.items()))

    pair = lax.ppermute(mine_pair, "space", [(i, i ^ 1) for i in range(bricks)])

    start_before = lax.ppermute(v, "tm", ring(slices, 1))

    q, keep, coarse, fields = pl.pallas_call(
        steps_kernel,
        in_specs=[vmem, anyspace, anyspace],
        out_specs=[vmem] * 4,
        out_shape=[
            out(FLAT, LANES),
            out(12 * NZ, LANES),
            out(4, ROWS, LANES),
            out(4 * FLAT, LANES),
        ],
        scratch_shapes=[pltpu.VMEM((FLAT + 2 * ROWS, LANES), f32)] * 2
        + [pltpu.SemaphoreType.DMA((8,))],
        name="steps",
    )(*inside(v), velocity.reshape(3 * FLAT, LANES), diffusivity.reshape(FLAT, LANES))
    fine, message, old, added = pl.pallas_call(
        lambda *refs: finish_kernel(bricks, *refs),
        in_specs=[vmem] * 7,
        out_specs=[vmem] * 4,
        out_shape=[
            out(FLAT, LANES),
            out(5, ROWS, LANES),
            out(ROWS, LANES),
            out(4 * NZ, LANES),
        ],
        name="finish",
    )(*inside(q, mine_pair, mine_cross, pair, cross, keep, coarse))

    chips = bricks // 2
    swap = [(i, i ^ 1) for i in range(bricks)]

    def send(value, group, k):
        pairs = []
        for i in range(bricks):
            to = 2 * ((i // 2 + 2 * group + i % 2) % chips) + i % 2
            pairs += [(i * slices + t, to * slices + (t + k) % slices) for t in range(slices)]
        return lax.ppermute(value, ("space", "tm"), pairs)

    partner = lax.ppermute(message, "space", swap)
    added = lax.ppermute(added, "tm", ring(slices, 1))
    earlier = pl.pallas_call(
        two_steps,
        in_specs=[vmem] * 2,
        out_specs=vmem,
        out_shape=out(FLAT, LANES),
        scratch_shapes=[pltpu.VMEM((FLAT + 2 * ROWS, LANES), f32)] * 2,
        name="steps_before",
    )(*inside(start_before, fields))
    both = jnp.concatenate([message, partner])
    tiles = jnp.stack([message[0], partner[0]])
    got = [
        send(both if k == slices - 1 else tiles, group, k)
        for group in range(pl.cdiv(chips, 2))
        for k in range(1, slices)
    ]
    got[0], earlier = lax.optimization_barrier((got[0], earlier))
    got = jnp.concatenate(got)
    swapped = lax.ppermute(got, "space", swap)

    corrected, jump = pl.pallas_call(
        lambda *refs: sweep_kernel(bricks, slices, *refs),
        in_specs=[vmem] * 9,
        out_specs=[vmem] * 2,
        out_shape=[jax.ShapeDtypeStruct((FLAT, LANES), f32)] * 2,
        scratch_shapes=[
            pltpu.VMEM((bricks, ROWS, LANES), f32),
            pltpu.VMEM((slices, bricks, ROWS, LANES), f32),
            pltpu.VMEM((bricks, 4, ROWS, LANES), f32),
        ],
        name="sweep",
    )(*inside(message, partner, got, swapped, fine, old, earlier, added, v))
    shape = (1, NZ, ROWS, LANES)
    return corrected.reshape(shape), jump.reshape(shape)


def solution(mesh):
    in_specs = (
        P(("groups", "tm"), None, "space", None),
        P(None, None, "space", None),
        P(None, "space", None),
    )
    out_specs = (P(("groups", "tm"), None, "space", None), P(("groups", "tm"), None, "space", None))
    return jax.shard_map(local, mesh=mesh, in_specs=in_specs, out_specs=out_specs, check_vma=False)
```

```python
import jax
import jax.numpy as jnp
from jax import lax
from jax.experimental import pallas as pl
from jax.experimental.pallas import tpu as pltpu
from jax.sharding import PartitionSpec as P

NZ, ROWS, LANES = 64, 8, 128
FLAT = NZ * ROWS
CHUNK = 16
EDGE = 3 * NZ + ROWS
BITS = ((0, 1), (0, 2), (1, 1), (1, 2))

f32 = jnp.float32


def shifted(x, by, axis):
    return pltpu.roll(x, (-by) % x.shape[axis], axis)


def iotas(shape):
    n = len(shape)
    return (
        lax.broadcasted_iota(jnp.int32, shape, n - 2),
        lax.broadcasted_iota(jnp.int32, shape, n - 1),
    )


def restrict_tile(planes):
    sub, lane = iotas((ROWS, LANES))
    for axis, dist in BITS:
        low = ((lane if axis else sub) // dist) % 2 == 0
        planes = [
            jnp.where(low, a + shifted(a, dist, axis), b + shifted(b, -dist, axis))
            for a, b in zip(planes[0::2], planes[1::2])
        ]
    return planes[0]


def prolong_tile(tile):
    sub, lane = iotas((ROWS, LANES))
    planes = [tile]
    for axis, dist in reversed(BITS):
        low = ((lane if axis else sub) // dist) % 2 == 0
        grown = []
        for a in planes:
            grown.append(jnp.where(low, a, shifted(a, -dist, axis)))
            grown.append(jnp.where(low, shifted(a, dist, axis), a))
        planes = grown
    return planes


def plane_sums(ref):
    def one(c):
        at = c * 4 * ROWS
        return (ref[at : at + ROWS] + ref[at + ROWS : at + 2 * ROWS]) + (
            ref[at + 2 * ROWS : at + 3 * ROWS] + ref[at + 3 * ROWS : at + 4 * ROWS]
        )

    return [one(c) for c in range(NZ // 4)]


def weights(cz, cx, cy, diff):
    out = []
    for c in (cz, cx, cy):
        out.append(diff + jnp.maximum(c, 0.0))
        out.append(diff - jnp.minimum(c, 0.0))
    centre = 1.0 - ((out[0] + out[1]) + (out[2] + out[3]) + (out[4] + out[5]))
    return out + [centre]


def row(ref, at):
    return ref[pl.ds(at, NZ, stride=ROWS), :]


def edges_kernel(v_hbm, vel_hbm, d_hbm, v_ref, pair_ref, cross_ref, face_ref, sems):
    copies = [pltpu.make_async_copy(v_hbm, v_ref, sems.at[0])]
    for side, face in enumerate((0, ROWS - 1)):
        for d in range(4):
            src = d_hbm if d == 3 else vel_hbm.at[d]
            j = 4 * side + d
            copies.append(pltpu.make_async_copy(src.at[:, face, :], face_ref.at[j], sems.at[1 + j]))
    for copy in copies:
        copy.start()
    odd = lax.axis_index("space") % 2 == 1
    for copy in copies:
        copy.wait()
    image = restrict_tile(plane_sums(v_ref)) * (1.0 / 64)
    for ref in (pair_ref, cross_ref):
        ref[3 * NZ : EDGE] = image
    sub, lane = iotas((NZ, LANES))
    rows = []
    for face, inner, side in ((0, 1, 0), (ROWS - 1, ROWS - 2, 1)):
        w = weights(*(face_ref[4 * side + d] for d in range(4)))
        v = row(v_ref, face)
        total = w[6] * v + w[3 - side] * row(v_ref, inner)
        total += jnp.where(sub == 0, 0.0, w[0]) * shifted(v, -1, 0)
        total += jnp.where(sub == NZ - 1, 0.0, w[1]) * shifted(v, 1, 0)
        total += jnp.where(lane == 0, 0.0, w[4]) * shifted(v, -1, 1)
        total += jnp.where(lane == LANES - 1, 0.0, w[5]) * shifted(v, 1, 1)
        rows.append((v, total, w[2 + side]))
    for j, (low, high) in enumerate(zip(*rows)):
        pair_ref[j * NZ : (j + 1) * NZ] = jnp.where(odd, low, high)
        cross_ref[j * NZ : (j + 1) * NZ] = jnp.where(odd, high, low)


def two_steps(v_ref, c_ref, q_ref, p_ref, pv_ref, waits=()):
    zero = jnp.zeros((ROWS, LANES), f32)
    for ref in (p_ref, pv_ref):
        ref[0:ROWS] = zero
        ref[FLAT + ROWS : FLAT + 2 * ROWS] = zero
    pv_ref[ROWS : FLAT + ROWS] = v_ref[...]
    shape = (CHUNK, ROWS, LANES)
    sub, lane = iotas(shape)
    size = CHUNK * ROWS

    def step(src, dst, dst_off):
        def body(c, carry):
            at = pl.multiple_of(c * size, size)
            load = lambda ref, off: ref[pl.ds(at + off, size), :].reshape(shape)
            w = weights(*(load(c_ref, d * FLAT) for d in range(4)))
            v = load(src, ROWS)
            total = w[6] * v + w[0] * load(src, 0) + w[1] * load(src, 2 * ROWS)
            total += jnp.where(sub == 0, 0.0, w[2]) * shifted(v, -1, 1)
            total += jnp.where(sub == ROWS - 1, 0.0, w[3]) * shifted(v, 1, 1)
            total += jnp.where(lane == 0, 0.0, w[4]) * shifted(v, -1, 2)
            total += jnp.where(lane == LANES - 1, 0.0, w[5]) * shifted(v, 1, 2)
            dst[pl.ds(at + dst_off, size), :] = total.reshape(size, LANES)
            return carry

        return lambda first, last: lax.fori_loop(first, last, body, 0)

    chunks = NZ // CHUNK
    first_step = step(pv_ref, p_ref, ROWS)
    for half, copies in enumerate(waits or ((), ())):
        for copy in copies:
            copy.wait()
        first_step(half * chunks // 2, (half + 1) * chunks // 2)
    step(p_ref, q_ref, 0)(0, chunks)


def steps_kernel(v_ref, vel_hbm, d_hbm, q_ref, keep_ref, coarse_ref, c_ref, p_ref, pv_ref, sems):
    copies = []
    for half in range(2):
        for d in range(4):
            src, at = (vel_hbm, d * FLAT) if d < 3 else (d_hbm, 0)
            at, to = at + half * FLAT // 2, d * FLAT + half * FLAT // 2
            copies.append(
                pltpu.make_async_copy(
                    src.at[pl.ds(at, FLAT // 2)], c_ref.at[pl.ds(to, FLAT // 2)], sems.at[4 * half + d]
                )
            )
    for copy in copies:
        copy.start()
    two_steps(v_ref, c_ref, q_ref, p_ref, pv_ref, (copies[:4], copies[4:]))
    for side, at in enumerate((0, ROWS - 1)):
        w = weights(*(row(c_ref, d * FLAT + at) for d in range(4)))
        for j, value in enumerate((w[0], w[1], w[4], w[5], w[6])):
            keep_ref[(side * 6 + j) * NZ : (side * 6 + j + 1) * NZ] = value
    keep_ref[5 * NZ : 6 * NZ] = row(c_ref, 3 * FLAT + 1) + jnp.maximum(row(c_ref, FLAT + 1), 0.0)
    keep_ref[11 * NZ : 12 * NZ] = row(c_ref, 3 * FLAT + ROWS - 2) - jnp.minimum(row(c_ref, FLAT + ROWS - 2), 0.0)
    for d, factor in enumerate((0.5, 0.5, 0.5, 0.125)):
        sums = restrict_tile(plane_sums(c_ref.at[d * FLAT : (d + 1) * FLAT]))
        coarse_ref[d] = sums * (factor / 64)


def coarse_weights(c, first, last):
    sub, lane = iotas((ROWS, LANES))
    zl, zh, y = sub % 4, lane % 4, lane // 4
    w = weights(c[0], c[1], c[2], c[3])
    w[0] = jnp.where((zl == 0) & (zh == 0), 0.0, w[0])
    w[1] = jnp.where((zl == 3) & (zh == 3), 0.0, w[1])
    w[4] = jnp.where(y == 0, 0.0, w[4])
    w[5] = jnp.where(y == LANES // 4 - 1, 0.0, w[5])
    w[2] = jnp.where((sub < 4) & first, 0.0, w[2])
    w[3] = jnp.where((sub >= 4) & last, 0.0, w[3])
    return w


def coarse_apply(w, v, own, lower, upper):
    sub, lane = iotas((ROWS, LANES))
    zl = sub % 4
    zb = jnp.where(zl == 0, shifted(shifted(v, -1, 1), 3, 0), shifted(v, -1, 0))
    za = jnp.where(zl == 3, shifted(shifted(v, 1, 1), -3, 0), shifted(v, 1, 0))
    xb = jnp.where(sub < 4, lower, own)
    xa = jnp.where(sub < 4, own, upper)
    return (
        (w[6] * v + w[0] * zb + w[1] * za)
        + (w[2] * xb + w[3] * xa)
        + (w[4] * shifted(v, -4, 1) + w[5] * shifted(v, 4, 1))
    )


def finish_kernel(bricks, q_ref, mine_pair_ref, mine_cross_ref, pair_ref, cross_ref, keep_ref, coarse_ref, fine_ref, message_ref, old_ref, added_ref):
    brick = lax.axis_index("space")
    odd = brick % 2 == 1
    has_low = brick > 0
    has_high = brick < bricks - 1
    part = lambda ref, j: ref[j * NZ : (j + 1) * NZ]

    def sides(pair, cross, j):
        a, b = part(pair, j), part(cross, j)
        return jnp.where(odd, a, b), jnp.where(odd, b, a)

    own = [sides(mine_pair_ref, mine_cross_ref, j) for j in (0, 2)]
    far = [sides(pair_ref, cross_ref, j) for j in range(3)]
    sub, lane = iotas((NZ, LANES))
    fine_ref[...] = q_ref[...]
    for side in range(2):
        wbz, waz, wby, way, centre, inner = (part(keep_ref, side * 6 + j) for j in range(6))
        k = jnp.where(has_high if side else has_low, own[1][side], 0.0)
        delta = k * far[0][side]
        beyond = far[1][side] + far[2][side] * own[0][side]
        edge = centre * delta + k * beyond
        edge += jnp.where(sub == 0, 0.0, wbz) * shifted(delta, -1, 0)
        edge += jnp.where(sub == NZ - 1, 0.0, waz) * shifted(delta, 1, 0)
        edge += jnp.where(lane == 0, 0.0, wby) * shifted(delta, -1, 1)
        edge += jnp.where(lane == LANES - 1, 0.0, way) * shifted(delta, 1, 1)
        e_at, i_at = (0, 1) if side == 0 else (ROWS - 1, ROWS - 2)
        for j, (at, extra) in enumerate(((e_at, edge), (i_at, inner * delta))):
            fine_ref[pl.ds(at, NZ, stride=ROWS), :] = row(q_ref, at) + extra
            added_ref[(2 * side + j) * NZ : (2 * side + j + 1) * NZ] = extra
    at = slice(3 * NZ, EDGE)
    v = mine_pair_ref[at]
    lower = jnp.where(odd, pair_ref[at], cross_ref[at])
    upper = jnp.where(odd, cross_ref[at], pair_ref[at])
    w = coarse_weights(coarse_ref, jnp.logical_not(has_low), jnp.logical_not(has_high))
    old = coarse_apply(w, v, *(shifted(x, 4, 0) for x in (v, lower, upper)))
    old_ref[...] = old
    image = restrict_tile(plane_sums(fine_ref)) * (1.0 / 64)
    message_ref[0] = jnp.where(lax.axis_index("tm") == 0, image, image - old)
    message_ref[1:5] = coarse_ref[...]


def sweep_kernel(bricks, slices, message_ref, partner_ref, got_ref, swapped_ref, fine_ref, old_ref, earlier_ref, added_ref, start_ref, corrected_ref, jump_ref, change_ref, tiles_ref, coef_ref):
    own, n = lax.axis_index("space"), lax.axis_index("tm")
    chips, chip, core = bricks // 2, own // 2, own % 2
    coef_ref[own] = message_ref[1:5]
    coef_ref[2 * chip + 1 - core] = partner_ref[1:5]
    for ref, c in ((got_ref, core), (swapped_ref, 1 - core)):
        at = 0
        for group in range(pl.cdiv(chips, 2)):
            source = (chip + 2 * chips - 2 * group - c) % chips
            for k in range(1, slices):
                for j in range(2):
                    brick = 2 * source + (c if j == 0 else 1 - c)
                    tiles_ref[k, brick] = ref[at]
                    if k == slices - 1:
                        coef_ref[brick] = ref[at + 1 : at + 5]
                    at += 5 if k == slices - 1 else 1
    w = [
        coarse_weights(coef_ref.at[b], b == 0, b == bricks - 1)
        for b in range(bricks)
    ]

    def coarse_step(m, image):
        c = [image[b] + tiles_ref[n - m, b] for b in range(bricks)]
        half = [shifted(v, 4, 0) for v in c]
        return tuple(
            coarse_apply(w[b], c[b], half[b], half[max(b - 1, 0)], half[min(b + 1, bricks - 1)])
            for b in range(bricks)
        )

    zero = tuple(jnp.zeros((ROWS, LANES), f32) for _ in range(bricks))
    image = lax.fori_loop(0, n, coarse_step, zero)
    for b in range(bricks):
        change_ref[b] = image[b]
    change = jnp.where(n == 0, 0.0, change_ref[own] - old_ref[...])
    planes = prolong_tile(change)
    for z in range(NZ):
        at = slice(z * ROWS, (z + 1) * ROWS)
        corrected_ref[at] = fine_ref[at] + planes[z // 4]
    keep = jnp.where(n == 0, 0.0, 1.0)
    jump_ref[...] = keep * (start_ref[...] - earlier_ref[...])
    for j, at in enumerate((0, 1, ROWS - 1, ROWS - 2)):
        extra = added_ref[j * NZ : (j + 1) * NZ]
        jump_ref[pl.ds(at, NZ, stride=ROWS), :] = row(jump_ref, at) - keep * extra


def local(start_states, velocity, diffusivity):
    bricks, slices = lax.axis_size("space"), lax.axis_size("tm")
    groups = lax.axis_size("groups")
    ring = lambda count, by: [(i, (i + by) % count) for i in range(count)]
    out = lambda *shape: pltpu.VMEM(shape, f32)
    vmem, anyspace = pl.BlockSpec(memory_space=pltpu.VMEM), pl.BlockSpec(memory_space=pl.ANY)
    inside = lambda *xs: [pltpu.with_memory_space_constraint(x, pltpu.VMEM) for x in xs]

    v, mine_pair, mine_cross = pl.pallas_call(
        edges_kernel,
        in_specs=[anyspace] * 3,
        out_specs=[vmem] * 3,
        out_shape=[
            out(FLAT, LANES),
            out(EDGE, LANES),
            out(EDGE, LANES),
        ],
        scratch_shapes=[pltpu.VMEM((8, NZ, LANES), f32), pltpu.SemaphoreType.DMA((9,))],
        name="edges",
    )(
        start_states.reshape(FLAT, LANES),
        velocity,
        diffusivity,
    )
    partner = {}
    for g in range(groups):
        for i in range(bricks):
            j, h = i + 1 if i % 2 else i - 1, g
            if j < 0 or j >= bricks:
                j, h = (i, g ^ 1) if groups % 2 == 0 else (j % bricks, g)
            partner[g * bricks + i] = h * bricks + j
    cross = lax.ppermute(mine_cross, ("groups", "space"), list(partner.items()))

    pair = lax.ppermute(mine_pair, "space", [(i, i ^ 1) for i in range(bricks)])

    start_before = lax.ppermute(v, "tm", ring(slices, 1))

    q, keep, coarse, fields = pl.pallas_call(
        steps_kernel,
        in_specs=[vmem, anyspace, anyspace],
        out_specs=[vmem] * 4,
        out_shape=[
            out(FLAT, LANES),
            out(12 * NZ, LANES),
            out(4, ROWS, LANES),
            out(4 * FLAT, LANES),
        ],
        scratch_shapes=[pltpu.VMEM((FLAT + 2 * ROWS, LANES), f32)] * 2
        + [pltpu.SemaphoreType.DMA((8,))],
        name="steps",
    )(*inside(v), velocity.reshape(3 * FLAT, LANES), diffusivity.reshape(FLAT, LANES))
    fine, message, old, added = pl.pallas_call(
        lambda *refs: finish_kernel(bricks, *refs),
        in_specs=[vmem] * 7,
        out_specs=[vmem] * 4,
        out_shape=[
            out(FLAT, LANES),
            out(5, ROWS, LANES),
            out(ROWS, LANES),
            out(4 * NZ, LANES),
        ],
        name="finish",
    )(*inside(q, mine_pair, mine_cross, pair, cross, keep, coarse))

    chips = bricks // 2
    swap = [(i, i ^ 1) for i in range(bricks)]

    def send(value, group, k):
        pairs = []
        for i in range(bricks):
            to = 2 * ((i // 2 + 2 * group + i % 2) % chips) + i % 2
            pairs += [(i * slices + t, to * slices + (t + k) % slices) for t in range(slices)]
        return lax.ppermute(value, ("space", "tm"), pairs)

    partner = lax.ppermute(message, "space", swap)
    added = lax.ppermute(added, "tm", ring(slices, 1))
    earlier = pl.pallas_call(
        two_steps,
        in_specs=[vmem] * 2,
        out_specs=vmem,
        out_shape=out(FLAT, LANES),
        scratch_shapes=[pltpu.VMEM((FLAT + 2 * ROWS, LANES), f32)] * 2,
        name="steps_before",
    )(*inside(start_before, fields))
    both = jnp.concatenate([message, partner])
    tiles = jnp.stack([message[0], partner[0]])
    got = [
        send(both if k == slices - 1 else tiles, group, k)
        for group in range(pl.cdiv(chips, 2))
        for k in range(1, slices)
    ]
    got[0], earlier = lax.optimization_barrier((got[0], earlier))
    got = jnp.concatenate(got)
    swapped = lax.ppermute(got, "space", swap)

    corrected, jump = pl.pallas_call(
        lambda *refs: sweep_kernel(bricks, slices, *refs),
        in_specs=[vmem] * 9,
        out_specs=[vmem] * 2,
        out_shape=[jax.ShapeDtypeStruct((FLAT, LANES), f32)] * 2,
        scratch_shapes=[
            pltpu.VMEM((bricks, ROWS, LANES), f32),
            pltpu.VMEM((slices, bricks, ROWS, LANES), f32),
            pltpu.VMEM((bricks, 4, ROWS, LANES), f32),
        ],
        name="sweep",
    )(*inside(message, partner, got, swapped, fine, old, earlier, added, v))
    shape = (1, NZ, ROWS, LANES)
    return corrected.reshape(shape), jump.reshape(shape)


def solution(mesh):
    in_specs = (
        P(("groups", "tm"), None, "space", None),
        P(None, None, "space", None),
        P(None, "space", None),
    )
    out_specs = (P(("groups", "tm"), None, "space", None), P(("groups", "tm"), None, "space", None))
    return jax.shard_map(local, mesh=mesh, in_specs=in_specs, out_specs=out_specs, check_vma=False)
```

```python
import jax
import jax.numpy as jnp
from jax import lax
from jax.experimental import pallas as pl
from jax.experimental.pallas import tpu as pltpu
from jax.sharding import PartitionSpec as P

NZ, ROWS, LANES = 64, 8, 128
FLAT = NZ * ROWS
CHUNK = 32
EDGE = 3 * NZ + ROWS
BITS = ((0, 1), (0, 2), (1, 1), (1, 2))

f32 = jnp.float32


def shifted(x, by, axis):
    return pltpu.roll(x, (-by) % x.shape[axis], axis)


def iotas(shape):
    n = len(shape)
    return (
        lax.broadcasted_iota(jnp.int32, shape, n - 2),
        lax.broadcasted_iota(jnp.int32, shape, n - 1),
    )


def restrict_tile(planes):
    sub, lane = iotas((ROWS, LANES))
    for axis, dist in BITS:
        low = ((lane if axis else sub) // dist) % 2 == 0
        planes = [
            jnp.where(low, a + shifted(a, dist, axis), b + shifted(b, -dist, axis))
            for a, b in zip(planes[0::2], planes[1::2])
        ]
    return planes[0]


def prolong_tile(tile):
    sub, lane = iotas((ROWS, LANES))
    planes = [tile]
    for axis, dist in reversed(BITS):
        low = ((lane if axis else sub) // dist) % 2 == 0
        grown = []
        for a in planes:
            grown.append(jnp.where(low, a, shifted(a, -dist, axis)))
            grown.append(jnp.where(low, shifted(a, dist, axis), a))
        planes = grown
    return planes


def plane_sums(ref):
    def one(c):
        at = c * 4 * ROWS
        return (ref[at : at + ROWS] + ref[at + ROWS : at + 2 * ROWS]) + (
            ref[at + 2 * ROWS : at + 3 * ROWS] + ref[at + 3 * ROWS : at + 4 * ROWS]
        )

    return [one(c) for c in range(NZ // 4)]


def weights(cz, cx, cy, diff):
    out = []
    for c in (cz, cx, cy):
        out.append(diff + jnp.maximum(c, 0.0))
        out.append(diff - jnp.minimum(c, 0.0))
    centre = 1.0 - ((out[0] + out[1]) + (out[2] + out[3]) + (out[4] + out[5]))
    return out + [centre]


def row(ref, at):
    return ref[pl.ds(at, NZ, stride=ROWS), :]


def edges_kernel(v_hbm, vel_hbm, d_hbm, v_ref, pair_ref, cross_ref, face_ref, sems):
    copies = [pltpu.make_async_copy(v_hbm, v_ref, sems.at[0])]
    for side, face in enumerate((0, ROWS - 1)):
        for d in range(4):
            src = d_hbm if d == 3 else vel_hbm.at[d]
            j = 4 * side + d
            copies.append(pltpu.make_async_copy(src.at[:, face, :], face_ref.at[j], sems.at[1 + j]))
    for copy in copies:
        copy.start()
    odd = lax.axis_index("space") % 2 == 1
    for copy in copies:
        copy.wait()
    image = restrict_tile(plane_sums(v_ref)) * (1.0 / 64)
    for ref in (pair_ref, cross_ref):
        ref[3 * NZ : EDGE] = image
    sub, lane = iotas((NZ, LANES))
    rows = []
    for face, inner, side in ((0, 1, 0), (ROWS - 1, ROWS - 2, 1)):
        w = weights(*(face_ref[4 * side + d] for d in range(4)))
        v = row(v_ref, face)
        total = w[6] * v + w[3 - side] * row(v_ref, inner)
        total += jnp.where(sub == 0, 0.0, w[0]) * shifted(v, -1, 0)
        total += jnp.where(sub == NZ - 1, 0.0, w[1]) * shifted(v, 1, 0)
        total += jnp.where(lane == 0, 0.0, w[4]) * shifted(v, -1, 1)
        total += jnp.where(lane == LANES - 1, 0.0, w[5]) * shifted(v, 1, 1)
        rows.append((v, total, w[2 + side]))
    for j, (low, high) in enumerate(zip(*rows)):
        pair_ref[j * NZ : (j + 1) * NZ] = jnp.where(odd, low, high)
        cross_ref[j * NZ : (j + 1) * NZ] = jnp.where(odd, high, low)


def two_steps(v_ref, c_ref, q_ref, p_ref, pv_ref, waits=()):
    zero = jnp.zeros((ROWS, LANES), f32)
    for ref in (p_ref, pv_ref):
        ref[0:ROWS] = zero
        ref[FLAT + ROWS : FLAT + 2 * ROWS] = zero
    pv_ref[ROWS : FLAT + ROWS] = v_ref[...]
    shape = (CHUNK, ROWS, LANES)
    sub, lane = iotas(shape)
    size = CHUNK * ROWS

    def step(src, dst, dst_off):
        def body(c, carry):
            at = pl.multiple_of(c * size, size)
            load = lambda ref, off: ref[pl.ds(at + off, size), :].reshape(shape)
            w = weights(*(load(c_ref, d * FLAT) for d in range(4)))
            v = load(src, ROWS)
            total = w[6] * v + w[0] * load(src, 0) + w[1] * load(src, 2 * ROWS)
            total += jnp.where(sub == 0, 0.0, w[2]) * shifted(v, -1, 1)
            total += jnp.where(sub == ROWS - 1, 0.0, w[3]) * shifted(v, 1, 1)
            total += jnp.where(lane == 0, 0.0, w[4]) * shifted(v, -1, 2)
            total += jnp.where(lane == LANES - 1, 0.0, w[5]) * shifted(v, 1, 2)
            dst[pl.ds(at + dst_off, size), :] = total.reshape(size, LANES)
            return carry

        return lambda first, last: lax.fori_loop(first, last, body, 0)

    chunks = NZ // CHUNK
    first_step = step(pv_ref, p_ref, ROWS)
    for half, copies in enumerate(waits or ((), ())):
        for copy in copies:
            copy.wait()
        first_step(half * chunks // 2, (half + 1) * chunks // 2)
    step(p_ref, q_ref, 0)(0, chunks)


def steps_kernel(v_ref, vel_hbm, d_hbm, q_ref, keep_ref, coarse_ref, c_ref, p_ref, pv_ref, sems):
    copies = []
    for half in range(2):
        for d in range(4):
            src, at = (vel_hbm, d * FLAT) if d < 3 else (d_hbm, 0)
            at, to = at + half * FLAT // 2, d * FLAT + half * FLAT // 2
            copies.append(
                pltpu.make_async_copy(
                    src.at[pl.ds(at, FLAT // 2)], c_ref.at[pl.ds(to, FLAT // 2)], sems.at[4 * half + d]
                )
            )
    for copy in copies:
        copy.start()
    two_steps(v_ref, c_ref, q_ref, p_ref, pv_ref, (copies[:4], copies[4:]))
    for side, at in enumerate((0, ROWS - 1)):
        w = weights(*(row(c_ref, d * FLAT + at) for d in range(4)))
        for j, value in enumerate((w[0], w[1], w[4], w[5], w[6])):
            keep_ref[(side * 6 + j) * NZ : (side * 6 + j + 1) * NZ] = value
    keep_ref[5 * NZ : 6 * NZ] = row(c_ref, 3 * FLAT + 1) + jnp.maximum(row(c_ref, FLAT + 1), 0.0)
    keep_ref[11 * NZ : 12 * NZ] = row(c_ref, 3 * FLAT + ROWS - 2) - jnp.minimum(row(c_ref, FLAT + ROWS - 2), 0.0)
    for d, factor in enumerate((0.5, 0.5, 0.5, 0.125)):
        sums = restrict_tile(plane_sums(c_ref.at[d * FLAT : (d + 1) * FLAT]))
        coarse_ref[d] = sums * (factor / 64)


def coarse_weights(c, first, last):
    sub, lane = iotas((ROWS, LANES))
    zl, zh, y = sub % 4, lane % 4, lane // 4
    w = weights(c[0], c[1], c[2], c[3])
    w[0] = jnp.where((zl == 0) & (zh == 0), 0.0, w[0])
    w[1] = jnp.where((zl == 3) & (zh == 3), 0.0, w[1])
    w[4] = jnp.where(y == 0, 0.0, w[4])
    w[5] = jnp.where(y == LANES // 4 - 1, 0.0, w[5])
    w[2] = jnp.where((sub < 4) & first, 0.0, w[2])
    w[3] = jnp.where((sub >= 4) & last, 0.0, w[3])
    return w


def coarse_apply(w, v, own, lower, upper):
    sub, lane = iotas((ROWS, LANES))
    zl = sub % 4
    zb = jnp.where(zl == 0, shifted(shifted(v, -1, 1), 3, 0), shifted(v, -1, 0))
    za = jnp.where(zl == 3, shifted(shifted(v, 1, 1), -3, 0), shifted(v, 1, 0))
    xb = jnp.where(sub < 4, lower, own)
    xa = jnp.where(sub < 4, own, upper)
    return (
        (w[6] * v + w[0] * zb + w[1] * za)
        + (w[2] * xb + w[3] * xa)
        + (w[4] * shifted(v, -4, 1) + w[5] * shifted(v, 4, 1))
    )


def finish_kernel(bricks, q_ref, mine_pair_ref, mine_cross_ref, pair_ref, cross_ref, keep_ref, coarse_ref, fine_ref, message_ref, old_ref, added_ref):
    brick = lax.axis_index("space")
    odd = brick % 2 == 1
    has_low = brick > 0
    has_high = brick < bricks - 1
    part = lambda ref, j: ref[j * NZ : (j + 1) * NZ]

    def sides(pair, cross, j):
        a, b = part(pair, j), part(cross, j)
        return jnp.where(odd, a, b), jnp.where(odd, b, a)

    own = [sides(mine_pair_ref, mine_cross_ref, j) for j in (0, 2)]
    far = [sides(pair_ref, cross_ref, j) for j in range(3)]
    sub, lane = iotas((NZ, LANES))
    fine_ref[...] = q_ref[...]
    for side in range(2):
        wbz, waz, wby, way, centre, inner = (part(keep_ref, side * 6 + j) for j in range(6))
        k = jnp.where(has_high if side else has_low, own[1][side], 0.0)
        delta = k * far[0][side]
        beyond = far[1][side] + far[2][side] * own[0][side]
        edge = centre * delta + k * beyond
        edge += jnp.where(sub == 0, 0.0, wbz) * shifted(delta, -1, 0)
        edge += jnp.where(sub == NZ - 1, 0.0, waz) * shifted(delta, 1, 0)
        edge += jnp.where(lane == 0, 0.0, wby) * shifted(delta, -1, 1)
        edge += jnp.where(lane == LANES - 1, 0.0, way) * shifted(delta, 1, 1)
        e_at, i_at = (0, 1) if side == 0 else (ROWS - 1, ROWS - 2)
        for j, (at, extra) in enumerate(((e_at, edge), (i_at, inner * delta))):
            fine_ref[pl.ds(at, NZ, stride=ROWS), :] = row(q_ref, at) + extra
            added_ref[(2 * side + j) * NZ : (2 * side + j + 1) * NZ] = extra
    at = slice(3 * NZ, EDGE)
    v = mine_pair_ref[at]
    lower = jnp.where(odd, pair_ref[at], cross_ref[at])
    upper = jnp.where(odd, cross_ref[at], pair_ref[at])
    w = coarse_weights(coarse_ref, jnp.logical_not(has_low), jnp.logical_not(has_high))
    old = coarse_apply(w, v, *(shifted(x, 4, 0) for x in (v, lower, upper)))
    old_ref[...] = old
    image = restrict_tile(plane_sums(fine_ref)) * (1.0 / 64)
    message_ref[0] = jnp.where(lax.axis_index("tm") == 0, image, image - old)
    message_ref[1:5] = coarse_ref[...]


def sweep_kernel(bricks, slices, message_ref, partner_ref, got_ref, swapped_ref, fine_ref, old_ref, earlier_ref, added_ref, start_ref, corrected_ref, jump_ref, change_ref, tiles_ref, coef_ref):
    own, n = lax.axis_index("space"), lax.axis_index("tm")
    chips, chip, core = bricks // 2, own // 2, own % 2
    coef_ref[own] = message_ref[1:5]
    coef_ref[2 * chip + 1 - core] = partner_ref[1:5]
    for ref, c in ((got_ref, core), (swapped_ref, 1 - core)):
        at = 0
        for group in range(pl.cdiv(chips, 2)):
            source = (chip + 2 * chips - 2 * group - c) % chips
            for k in range(1, slices):
                for j in range(2):
                    brick = 2 * source + (c if j == 0 else 1 - c)
                    tiles_ref[k, brick] = ref[at]
                    if k == slices - 1:
                        coef_ref[brick] = ref[at + 1 : at + 5]
                    at += 5 if k == slices - 1 else 1
    w = [
        coarse_weights(coef_ref.at[b], b == 0, b == bricks - 1)
        for b in range(bricks)
    ]

    def coarse_step(m, image):
        c = [image[b] + tiles_ref[n - m, b] for b in range(bricks)]
        half = [shifted(v, 4, 0) for v in c]
        return tuple(
            coarse_apply(w[b], c[b], half[b], half[max(b - 1, 0)], half[min(b + 1, bricks - 1)])
            for b in range(bricks)
        )

    zero = tuple(jnp.zeros((ROWS, LANES), f32) for _ in range(bricks))
    image = lax.fori_loop(0, n, coarse_step, zero)
    for b in range(bricks):
        change_ref[b] = image[b]
    change = jnp.where(n == 0, 0.0, change_ref[own] - old_ref[...])
    planes = prolong_tile(change)
    for z in range(NZ):
        at = slice(z * ROWS, (z + 1) * ROWS)
        corrected_ref[at] = fine_ref[at] + planes[z // 4]
    keep = jnp.where(n == 0, 0.0, 1.0)
    jump_ref[...] = keep * (start_ref[...] - earlier_ref[...])
    for j, at in enumerate((0, 1, ROWS - 1, ROWS - 2)):
        extra = added_ref[j * NZ : (j + 1) * NZ]
        jump_ref[pl.ds(at, NZ, stride=ROWS), :] = row(jump_ref, at) - keep * extra


def local(start_states, velocity, diffusivity):
    bricks, slices = lax.axis_size("space"), lax.axis_size("tm")
    groups = lax.axis_size("groups")
    ring = lambda count, by: [(i, (i + by) % count) for i in range(count)]
    out = lambda *shape: pltpu.VMEM(shape, f32)
    vmem, anyspace = pl.BlockSpec(memory_space=pltpu.VMEM), pl.BlockSpec(memory_space=pl.ANY)
    inside = lambda *xs: [pltpu.with_memory_space_constraint(x, pltpu.VMEM) for x in xs]

    v, mine_pair, mine_cross = pl.pallas_call(
        edges_kernel,
        in_specs=[anyspace] * 3,
        out_specs=[vmem] * 3,
        out_shape=[
            out(FLAT, LANES),
            out(EDGE, LANES),
            out(EDGE, LANES),
        ],
        scratch_shapes=[pltpu.VMEM((8, NZ, LANES), f32), pltpu.SemaphoreType.DMA((9,))],
        name="edges",
    )(
        start_states.reshape(FLAT, LANES),
        velocity,
        diffusivity,
    )
    partner = {}
    for g in range(groups):
        for i in range(bricks):
            j, h = i + 1 if i % 2 else i - 1, g
            if j < 0 or j >= bricks:
                j, h = (i, g ^ 1) if groups % 2 == 0 else (j % bricks, g)
            partner[g * bricks + i] = h * bricks + j
    cross = lax.ppermute(mine_cross, ("groups", "space"), list(partner.items()))

    pair = lax.ppermute(mine_pair, "space", [(i, i ^ 1) for i in range(bricks)])

    start_before = lax.ppermute(v, "tm", ring(slices, 1))

    q, keep, coarse, fields = pl.pallas_call(
        steps_kernel,
        in_specs=[vmem, anyspace, anyspace],
        out_specs=[vmem] * 4,
        out_shape=[
            out(FLAT, LANES),
            out(12 * NZ, LANES),
            out(4, ROWS, LANES),
            out(4 * FLAT, LANES),
        ],
        scratch_shapes=[pltpu.VMEM((FLAT + 2 * ROWS, LANES), f32)] * 2
        + [pltpu.SemaphoreType.DMA((8,))],
        name="steps",
    )(*inside(v), velocity.reshape(3 * FLAT, LANES), diffusivity.reshape(FLAT, LANES))
    fine, message, old, added = pl.pallas_call(
        lambda *refs: finish_kernel(bricks, *refs),
        in_specs=[vmem] * 7,
        out_specs=[vmem] * 4,
        out_shape=[
            out(FLAT, LANES),
            out(5, ROWS, LANES),
            out(ROWS, LANES),
            out(4 * NZ, LANES),
        ],
        name="finish",
    )(*inside(q, mine_pair, mine_cross, pair, cross, keep, coarse))

    chips = bricks // 2
    swap = [(i, i ^ 1) for i in range(bricks)]

    def send(value, group, k):
        pairs = []
        for i in range(bricks):
            to = 2 * ((i // 2 + 2 * group + i % 2) % chips) + i % 2
            pairs += [(i * slices + t, to * slices + (t + k) % slices) for t in range(slices)]
        return lax.ppermute(value, ("space", "tm"), pairs)

    partner = lax.ppermute(message, "space", swap)
    added = lax.ppermute(added, "tm", ring(slices, 1))
    earlier = pl.pallas_call(
        two_steps,
        in_specs=[vmem] * 2,
        out_specs=vmem,
        out_shape=out(FLAT, LANES),
        scratch_shapes=[pltpu.VMEM((FLAT + 2 * ROWS, LANES), f32)] * 2,
        name="steps_before",
    )(*inside(start_before, fields))
    both = jnp.concatenate([message, partner])
    tiles = jnp.stack([message[0], partner[0]])
    got = [
        send(both if k == slices - 1 else tiles, group, k)
        for group in range(pl.cdiv(chips, 2))
        for k in range(1, slices)
    ]
    got[0], earlier = lax.optimization_barrier((got[0], earlier))
    got = jnp.concatenate(got)
    swapped = lax.ppermute(got, "space", swap)

    corrected, jump = pl.pallas_call(
        lambda *refs: sweep_kernel(bricks, slices, *refs),
        in_specs=[vmem] * 9,
        out_specs=[vmem] * 2,
        out_shape=[jax.ShapeDtypeStruct((FLAT, LANES), f32)] * 2,
        scratch_shapes=[
            pltpu.VMEM((bricks, ROWS, LANES), f32),
            pltpu.VMEM((slices, bricks, ROWS, LANES), f32),
            pltpu.VMEM((bricks, 4, ROWS, LANES), f32),
        ],
        name="sweep",
    )(*inside(message, partner, got, swapped, fine, old, earlier, added, v))
    shape = (1, NZ, ROWS, LANES)
    return corrected.reshape(shape), jump.reshape(shape)


def solution(mesh):
    in_specs = (
        P(("groups", "tm"), None, "space", None),
        P(None, None, "space", None),
        P(None, "space", None),
    )
    out_specs = (P(("groups", "tm"), None, "space", None), P(("groups", "tm"), None, "space", None))
    return jax.shard_map(local, mesh=mesh, in_specs=in_specs, out_specs=out_specs, check_vma=False)
```
